32 devices in a mesh: dp: 2 (over x), seq: 16 (over z, y, core).
Axes of the slice: x: 2, y: 2, z: 4, core: 2. Of those that a mesh axis runs over, the one named last changes fastest.
Arguments:
- tokens: bfloat16 [2, 2048, 1536], P('dp', 'seq'), may hold values from -6 to 6
- query_weight: bfloat16 [1536, 1024], P('seq'), may hold values from -0.15564466 to 0.15564466
- key_weight: bfloat16 [1536, 128], P('seq'), may hold values from -7.6546554 to 7.6546554
- value_weight: bfloat16 [1536, 128], P('seq'), may hold values from -0.15625 to 0.15625
- output_weight: bfloat16 [1536, 1024], P('seq'), may hold values from -0.1875 to 0.1875
- row_weight: bfloat16 [1536, 128], replicated, may hold values from -0.15625 to 0.15625
- col_weight: bfloat16 [1536, 128], replicated, may hold values from -0.15625 to 0.15625
- pair_cotangent: bfloat16 [2, 128, 128, 128], P('dp', 'seq'), may hold values from -0.046875 to 0.046875
Outputs:
- pair: bfloat16 [2, 128, 128, 128], P('dp', 'seq')
- grad_row_weight: bfloat16 [1536, 128], replicated
- grad_col_weight: bfloat16 [1536, 128], replicated
The draws below stay inside these ranges and needn't reach their ends.
All inputs are finite; a program needn't handle non-finite values.
Results may differ from the reference program's by a relative error of at most 0.025.
The reference program's roundings to bfloat16 on the way (of `normed`, `rounded`, `attended` and `bin_feat`) count: a program that leaves them out, or rounds other values in their place, can miss the bound.
Values may be sent and summed in bfloat16 or wider, within the bound.
A program may use at most 64 MiB of HBM per device.

```python
import math
import jax
import jax.numpy as jnp
from jax import lax

D = 1536
HEADS = 8
HD = 128
PAIR_C = 128
POOL = 16
SEQ_LEN = 2048
BINS = 128
SAMPLES = 2


def shared_query(key):
    base = jax.random.truncated_normal(jax.random.fold_in(key, 11), -6.0, 6.0, (D, HEADS * HD), jnp.float32)
    return base / math.sqrt(D)


def draw_query_weight(key, part):
    return shared_query(key).astype(jnp.bfloat16)


def draw_key_weight(key, part):
    noise = jax.random.truncated_normal(jax.random.fold_in(key, 12), -6.0, 6.0, (D, HD), jnp.float32) / math.sqrt(D)
    return noise.astype(jnp.bfloat16)


def draw_tokens(key, part):
    base = jax.random.truncated_normal(jax.random.fold_in(key, 21), -6.0, 6.0, (SAMPLES, SEQ_LEN, D), jnp.float32)
    return base.astype(jnp.bfloat16)


def with_spikes(entries, key, source, target, parts, factor):
    def block_of(dim):
        return (jnp.arange(entries.shape[dim]) // (entries.shape[dim] // parts)).reshape((-1,) + (1,) * (entries.ndim - 1 - dim))

    near = jax.random.permutation(key, parts)[block_of(target)]
    second = (block_of(target) + parts // 2) % parts
    return jnp.where((block_of(source) == near) | (block_of(source) == second), factor * entries, entries)


def block_levels(own_key, dims, pieces, smallest, largest):
    level, own = 1.0, jax.random.fold_in(own_key, 6)
    for dim, shards_of in pieces:
        heights = jnp.exp(jax.random.uniform(jax.random.fold_in(own, dim), (shards_of,), jnp.float32, smallest / len(pieces), largest / len(pieces)))
        level = level * jnp.repeat(heights, dims[dim] // shards_of).reshape([-1 if axis == dim else 1 for axis in range(len(dims))])
    return level


def centred(stream_key, shape, deviation, limit, shards=(), dtype=jnp.bfloat16):
    gain = block_levels(stream_key, shape, shards, -0.22, 0.18) if shards else 1.0
    array = jax.random.normal(stream_key, shape, jnp.float32) * deviation * gain
    return jnp.minimum(jnp.maximum(array, -limit), limit).astype(dtype)


def heavy_noise(rng, dims, scale, most, cuts, heavy, dtype=jnp.bfloat16):
    entries = scale * jax.random.normal(rng, dims, jnp.float32)
    if cuts:
        entries = entries * block_levels(rng, dims, cuts, -0.22, 0.18)
    return jnp.clip(with_spikes(entries, jax.random.fold_in(rng, 3), *heavy), -most, most).astype(dtype)


def setup_inputs(seed: int = 0) -> dict:
    seeds = jax.random.split(jax.random.key(seed), 9)
    tokens = draw_tokens(jax.random.fold_in(seeds[8], 71), 0)
    query_weight = draw_query_weight(jax.random.fold_in(seeds[8], 71), 0)
    key_weight = draw_key_weight(jax.random.fold_in(seeds[8], 71), 0)
    value_weight = centred(seeds[3], (D, HD), D ** -0.5, 0.15625, ((0, 16),))
    output_weight = centred(seeds[4], (D, HEADS * HD), (HEADS * HD) ** -0.5, 0.1875, ((0, 16),))
    row_weight = centred(seeds[5], (D, PAIR_C), D ** -0.5, 0.15625)
    col_weight = centred(seeds[6], (D, PAIR_C), D ** -0.5, 0.15625)
    pair_cotangent = heavy_noise(seeds[7], (SAMPLES, BINS, BINS, PAIR_C), (1.0 / BINS), 0.046875, ((0, 2), (1, 16)), (1, 2, 16, 2.0))
    return dict(tokens=tokens, query_weight=query_weight, key_weight=key_weight, value_weight=value_weight, output_weight=output_weight, row_weight=row_weight, col_weight=col_weight, pair_cotangent=pair_cotangent)


def rms_rows(values):
    return values * lax.rsqrt(lax.optimization_barrier(jnp.mean(values * values, axis=-1, keepdims=True)) + 1e-06)

def one_sample(tokens, cotangent, query_weight, key_weight, value_weight, output_weight, row_weight, col_weight):
    normed = rms_rows(tokens.astype(jnp.float32)).astype(jnp.bfloat16)
    queries = jnp.dot(normed, query_weight, preferred_element_type=jnp.float32).astype(jnp.bfloat16)
    keys = jnp.dot(normed, key_weight, preferred_element_type=jnp.float32).astype(jnp.bfloat16)
    values = jnp.dot(normed, value_weight, preferred_element_type=jnp.float32).astype(jnp.bfloat16)
    keys_wide = keys.astype(jnp.float32)
    values_wide = values.astype(jnp.float32)
    rows_all = SEQ_LEN * HEADS
    block = math.gcd(1024, rows_all)
    query_rows = queries.reshape(rows_all // block, block, HD).astype(jnp.float32)
    scale = 1.0 / math.sqrt(HD)

    def attend(query_block):
        scores = jnp.dot(query_block, keys_wide.T) * scale
        weights = jnp.exp(scores - lax.optimization_barrier(jnp.max(scores, axis=1, keepdims=True)))
        total = lax.optimization_barrier(jnp.sum(weights, axis=1, keepdims=True))
        rounded = weights.astype(jnp.bfloat16).astype(jnp.float32)
        return (jnp.dot(rounded, values_wide) / total).astype(jnp.bfloat16)
    attended = lax.map(attend, query_rows).reshape(SEQ_LEN, HEADS * HD)
    update = jnp.dot(attended.astype(jnp.float32), output_weight.astype(jnp.float32).T)
    pooled = lax.optimization_barrier(jnp.mean(update.reshape(BINS, POOL, D), axis=1))
    bin_feat = rms_rows(pooled).astype(jnp.bfloat16)
    row_proj = jnp.dot(bin_feat, row_weight, preferred_element_type=jnp.float32).astype(jnp.bfloat16)
    col_proj = jnp.dot(bin_feat, col_weight, preferred_element_type=jnp.float32).astype(jnp.bfloat16)
    row_wide = row_proj.astype(jnp.float32)
    col_wide = col_proj.astype(jnp.float32)
    pair = (row_wide[:, None, :] * col_wide[None, :, :]).astype(jnp.bfloat16)
    cot_wide = cotangent.astype(jnp.float32)
    row_grad = jnp.einsum('ijc,jc->ic', cot_wide, col_wide).astype(jnp.bfloat16)
    col_grad = jnp.einsum('ijc,ic->jc', cot_wide, row_wide).astype(jnp.bfloat16)
    feat_wide = bin_feat.astype(jnp.float32)
    grad_row = jnp.dot(feat_wide.T, row_grad.astype(jnp.float32))
    grad_col = jnp.dot(feat_wide.T, col_grad.astype(jnp.float32))
    return (pair, grad_row, grad_col)

def reference(tokens, query_weight, key_weight, value_weight, output_weight, row_weight, col_weight, pair_cotangent):
    pairs = []
    grad_row = jnp.zeros((D, PAIR_C), jnp.float32)
    grad_col = jnp.zeros((D, PAIR_C), jnp.float32)
    for sample in range(SAMPLES):
        pair, g_row, g_col = one_sample(tokens[sample], pair_cotangent[sample], query_weight, key_weight, value_weight, output_weight, row_weight, col_weight)
        pairs.append(pair)
        grad_row = grad_row + g_row
        grad_col = grad_col + g_col
    return (jnp.stack(pairs, 0), grad_row.astype(jnp.bfloat16), grad_col.astype(jnp.bfloat16))
```

```python
import functools
import math

import jax
import jax.numpy as jnp
from jax import lax
from jax.experimental import pallas as pl
from jax.experimental.pallas import tpu as pltpu
from jax.sharding import PartitionSpec as P

POOL = 16
LINE = 4
ORDER = (1, LINE - 1, *range(2, LINE - 1))
F32 = jnp.float32
BF16 = jnp.bfloat16
MESH = pl.DeviceIdType.MESH
LAST = (((1,), (1,)), ((), ()))


def merge_rows(block, rows):
    if block.shape[1] % 16 == 0:
        return block.reshape(rows, block.shape[2])
    return block.astype(F32).reshape(rows, block.shape[2]).astype(block.dtype)


class Where:
    def __init__(self, n_dp, n_seq):
        self.n_dp, self.n_seq = n_dp, n_seq
        self.mid = n_seq // (LINE * 2)
        self.chips = n_seq // 2
        self.dp, self.me = lax.axis_index("dp"), lax.axis_index("seq")
        self.core = self.me % 2
        self.y = (self.me // 2) % self.mid
        self.z = self.me // (2 * self.mid)
        self.sibling = self.at(0, 0, True)

    def at(self, dz, dy, flip):
        z = (self.z + dz) % LINE
        y = (self.y + dy) % self.mid
        core = 1 - self.core if flip else self.core
        return (z * self.mid + y) * 2 + core

    def send(self, src, dst, send_sem, recv_sem, peer, dp=None):
        copy = pltpu.make_async_remote_copy(
            src_ref=src,
            dst_ref=dst,
            send_sem=send_sem,
            recv_sem=recv_sem,
            device_id=(self.dp if dp is None else dp, peer),
            device_id_type=MESH,
        )
        copy.start()

    def landed(self, ref, sem):
        pltpu.make_async_copy(ref, ref, sem).wait()


class Halves:
    def __init__(self, where, own, slot, send_sem, recv_sem):
        self.w, self.own, self.slot = where, own, slot
        self.send_sem, self.recv_sem = send_sem, recv_sem

    def give(self, peer, flip):
        w = self.w
        src = self.own(1 - w.core if flip else w.core)
        w.send(src, self.slot(w.me), self.send_sem, self.recv_sem.at[w.me], peer)

    def start_line(self):
        for dz in ORDER:
            for flip in (False, True):
                self.give(self.w.at(dz, 0, flip), flip)

    def start_mid(self):
        for dy in range(1, self.w.mid):
            for flip in (False, True):
                self.give(self.w.at(0, dy, flip), flip)

    def arrived(self, block):
        self.w.landed(self.slot(block), self.recv_sem.at[block])

    def hold(self, block):
        pass

    def pass_line(self):
        w = self.w
        for dz in ORDER:
            for flip in (False, True):
                block = w.at(dz, 0, flip)
                self.arrived(block)
                for dy in range(1, w.mid):
                    ref = self.slot(block)
                    w.send(ref, ref, self.send_sem, self.recv_sem.at[block], w.at(0, dy, False))
                self.hold(block)

    def pass_mid(self):
        w = self.w
        for dz in (0, *ORDER):
            for dy in range(1, w.mid):
                for flip in (False, True):
                    block = w.at(dz, dy, flip)
                    self.arrived(block)
                    self.hold(block)


class Traded(Halves):
    def __init__(self, where, own, slot, send_sem, recv_sem, trade, x_send, x_recv):
        super().__init__(where, own, slot, send_sem, recv_sem)
        self.trade, self.x_send, self.x_recv = trade, x_send, x_recv

    def hold(self, block):
        w = self.w
        odd = w.dp % 2
        ref = self.trade(block, odd)
        w.send(ref, ref, self.x_send, self.x_recv.at[block], w.me, w.dp + 1 - 2 * odd)

    def pass_across(self):
        w = self.w
        for dy in range(w.mid):
            for dz in (0, *ORDER):
                if dz or dy:
                    for flip in (False, True):
                        block = w.at(dz, dy, flip)
                        w.landed(self.trade(block, 1 - w.dp % 2), self.x_recv.at[block])


class Gather:
    def __init__(self, where, slot, send_sem, recv_sem):
        self.w, self.slot = where, slot
        self.send_sem, self.recv_sem = send_sem, recv_sem

    def push(self, block, peer, flip):
        ref = self.slot(block)
        sem = self.send_sem.at[1 if flip else 0]
        self.w.send(ref, ref, sem, self.recv_sem.at[block], peer)

    def arrived(self, block):
        self.w.landed(self.slot(block), self.recv_sem.at[block])

    def start(self):
        w = self.w
        for dz in ORDER:
            self.push(w.me, w.at(dz, 0, False), False)
        self.spread(0)

    def spread(self, dz):
        w = self.w
        block = w.at(dz, 0, False)
        for dy in range(1, w.mid):
            self.push(block, w.at(0, dy, False), False)
        self.push(block, w.sibling, True)

    def pass_line(self):
        for dz in ORDER:
            self.arrived(self.w.at(dz, 0, False))
            self.spread(dz)

    def pass_mid(self, dy):
        w = self.w
        for dz in (0, *ORDER):
            block = w.at(dz, dy, False)
            self.arrived(block)
            self.push(block, w.sibling, True)

    def complete(self):
        w = self.w
        for dz in (0, *ORDER):
            for dy in range(w.mid):
                self.arrived(w.at(dz, dy, True))


def each(total, act):
    def step(k, unused):
        act(k)
        return unused

    lax.fori_loop(0, total, step, 0)


def main_kernel(
    n_dp,
    n_seq,
    share,
    tok_hbm,
    wq_hbm,
    wk_hbm,
    wv_hbm,
    wo_hbm,
    roww_hbm,
    colw_hbm,
    cot_hbm,
    rowp_out,
    colp_out,
    turned_out,
    grads_out,
    rowp_ref,
    colp_ref,
    turned,
    grads,
    tok_ref,
    pairw_ref,
    cot_ref,
    pack,
    cot_in,
    wkv_own,
    wkv_buf,
    wq_own,
    wq_buf,
    wo_own,
    wo_buf,
    normed_ref,
    kv_ref,
    binned,
    part_ref,
    part_in,
    pool_ref,
    load_sem,
    save_sem,
    wkv_recv,
    wq_recv,
    x_recv,
    kv_recv,
    bin_send,
    bin_recv,
    pool_recv,
    group_recv,
    sems,
):
    w = Where(n_dp, n_seq)
    dp, me, core, chips, mid = w.dp, w.me, w.core, w.chips, w.mid
    every = n_dp * n_seq
    flat = dp * n_seq + me
    head = wk_hbm.shape[2]
    half = wq_own.shape[3]
    heads = half // head
    rows, width = tok_ref.shape
    bins, count = cot_ref.shape[0:2]
    pieces = wq_own.shape[1]
    shard = width // n_seq
    sem = iter(range(sems.shape[0]))
    one = lambda: sems.at[next(sem)]

    sources = [
        (tok_hbm, tok_ref),
        (wk_hbm, wkv_own.at[0]),
        (wv_hbm, wkv_own.at[1]),
        (wq_hbm.at[:, :, pl.ds(0, half)], wq_own.at[0]),
        (wq_hbm.at[:, :, pl.ds(half, half)], wq_own.at[1]),
        (wo_hbm.at[:, :, pl.ds(0, half)], wo_own.at[0]),
        (wo_hbm.at[:, :, pl.ds(half, half)], wo_own.at[1]),
        (cot_hbm, cot_ref),
        (roww_hbm, pairw_ref.at[:, pl.ds(0, head)]),
        (colw_hbm, pairw_ref.at[:, pl.ds(head, head)]),
    ]
    loads = [
        pltpu.make_async_copy(src, dst, load_sem.at[i]) for i, (src, dst) in enumerate(sources)
    ]
    for load in loads:
        load.start()

    barrier = pltpu.get_barrier_semaphore()

    def greet(k):
        peer = (flat + k + 1) % every
        pl.semaphore_signal(
            barrier, inc=1, device_id=(peer // n_seq, peer % n_seq), device_id_type=MESH
        )

    each(every - 1, greet)
    loads[0].wait()
    tok = tok_ref[...].astype(F32)
    normed_ref[core] = (
        tok * lax.rsqrt(jnp.mean(tok * tok, axis=1, keepdims=True) + 1e-06)
    ).astype(BF16)
    for load in loads[1:5]:
        load.wait()

    odd = dp % 2
    wkv_send, wq_send, x_send = one(), one(), one()
    wkv = Halves(w, lambda c: wkv_own.at[c], lambda s: wkv_buf.at[s], wkv_send, wkv_recv)
    kept = lambda s: wq_buf.at[s, pl.ds(odd * (pieces - share), share)]
    wq = Traded(
        w,
        lambda c: wq_own.at[c, pl.ds(odd * (pieces - share), share)],
        kept,
        wq_send,
        wq_recv,
        lambda s, o: wq_buf.at[s, pl.ds(o * share, pieces - share)],
        x_send,
        x_recv,
    )

    pl.semaphore_wait(barrier, every - 1)
    wkv.start_line()
    wkv.start_mid()
    wkv.give(w.sibling, True)
    normed_send, normed_recv = one(), one()
    w.send(normed_ref.at[core], normed_ref.at[core], normed_send, normed_recv, w.sibling)
    wq.start_line()
    wq_beside = one()
    w.send(wq_own.at[1 - core], wq_buf.at[me], wq_beside, wq_recv.at[me], w.sibling)
    wkv_buf[me] = wkv_own[core]
    wq_buf[me] = wq_own[core]
    wkv.pass_line()
    wq.start_mid()
    loads[5].wait()
    loads[6].wait()
    wo_send, wo_recv = one(), one()
    w.send(wo_own.at[1 - core], wo_buf.at[core], wo_send, wo_recv, w.sibling)
    wo_buf[core] = wo_own[core]
    w.landed(normed_ref.at[1 - core], normed_recv)
    normed = normed_ref[...].reshape(2 * rows, width)
    wkv.pass_mid()
    wkv.arrived(w.sibling)

    def whole(buf):
        return merge_rows(
            buf[...].reshape(n_seq * buf.shape[1], buf.shape[2], buf.shape[3]), width
        )

    kv_ref[core, me // 2] = jnp.dot(
        normed, whole(wkv_buf), preferred_element_type=F32
    ).astype(BF16)
    kv_sends = (one(), one())

    class Sends:
        def __init__(self, pair):
            self.at = pair

    blocks = Gather(w, lambda s: kv_ref.at[s % 2, s // 2], Sends(kv_sends), kv_recv)
    blocks.start()
    wq.pass_line()
    blocks.pass_line()
    wq.pass_mid()
    for dy in range(1, mid):
        blocks.pass_mid(dy)

    loads[7].wait()
    squares = cot_ref[...].astype(F32)
    for p in range(n_seq):
        pack[p] = jnp.concatenate(
            [squares[i, p * bins : (p + 1) * bins] for i in range(bins)], axis=0
        ).astype(BF16)
    cot_in[me] = pack[me]

    wq.pass_across()
    w.landed(wq_buf.at[w.sibling], wq_recv.at[w.sibling])
    queries = jnp.dot(normed, whole(wq_buf), preferred_element_type=F32).astype(BF16)
    blocks.complete()

    cot_send, cot_recv = one(), one()

    def turn(k):
        peer = (me + k + 1) % n_seq
        w.send(pack.at[peer], cot_in.at[me], cot_send, cot_recv, peer)

    each(n_seq - 1, turn)

    keys = kv_ref[0].reshape(n_seq * rows, head)
    values = kv_ref[1].reshape(n_seq * rows, head)
    factor = math.log2(math.e) / math.sqrt(head)
    chip_bins = 2 * bins
    for h in range(heads):
        scores = lax.dot_general(
            queries[:, h * head : (h + 1) * head], keys, LAST, preferred_element_type=F32
        )
        top = jnp.max(scores, axis=1, keepdims=True)
        weights = jnp.exp2((scores - top) * factor)
        total = jnp.sum(weights, axis=1, keepdims=True)
        out = jnp.dot(weights.astype(BF16), values, preferred_element_type=F32) / total
        out = out.astype(BF16).astype(F32)
        binned[h, me // 2] = jnp.sum(out.reshape(chip_bins, POOL, head), axis=1).astype(BF16)
        ref = binned.at[h, me // 2]
        for dy in range(mid):
            for dz in (2, 1, 3, 0):
                if dz or dy:
                    w.send(ref, ref, bin_send.at[h], bin_recv.at[h], w.at(dz, dy, False))

    for load in loads[8:]:
        load.wait()
    w.landed(wo_buf.at[1 - core], wo_recv)
    wo = merge_rows(
        wo_buf[...].reshape(2 * wo_buf.shape[1], wo_buf.shape[2], half), 2 * shard
    )
    partial = jnp.zeros((2 * shard, count), F32)
    for h in range(heads):
        w.landed(binned.at[h, pl.ds(0, chips - 1)], bin_recv.at[h])
        partial = partial + lax.dot_general(
            wo[:, h * head : (h + 1) * head],
            binned[h].reshape(count, head),
            LAST,
            preferred_element_type=F32,
        )
    part_ref[0] = partial[0:shard]
    part_ref[1] = partial[shard : 2 * shard]
    part_send, part_recv = one(), one()
    w.send(part_ref.at[1 - core], part_in, part_send, part_recv, w.sibling)
    w.landed(part_in, part_recv)
    pooled = (part_ref[core] + part_in[...]) * (1.0 / POOL)
    spot = lambda s: ((s // 2) % mid) * LINE + s // (2 * mid)
    pool_ref[dp, core, spot(me)] = pooled.reshape(pool_ref.shape[3:]).astype(BF16)
    own = Gather(
        w, lambda s: pool_ref.at[dp, s % 2, spot(s)], Sends((one(), one())), pool_recv
    )
    own.start()
    across_send, beside_send = one(), one()

    def group(p, c, y):
        return pool_ref.at[p, c, pl.ds(y * LINE, LINE)]

    def across(y):
        for d in range(1, n_dp):
            ref = group(dp, core, y)
            w.send(ref, ref, across_send, group_recv.at[dp, core, y], me, (dp + d) % n_dp)

    own.pass_line()
    across(w.y)
    for dy in range(1, mid):
        own.pass_mid(dy)
        across((w.y + dy) % mid)
    own.complete()

    def features(p):
        stacked = jnp.concatenate(
            [
                pool_ref[p, c, y * LINE + z].astype(F32).reshape(shard, count)
                for z in range(LINE)
                for y in range(mid)
                for c in range(2)
            ],
            axis=0,
        )
        scale = lax.rsqrt(jnp.mean(stacked * stacked, axis=0, keepdims=True) + 1e-06)
        return (stacked * scale).astype(BF16)

    def save(src, dst, i):
        copy = pltpu.make_async_copy(src, dst, save_sem.at[i])
        copy.start()
        return copy

    feat = features(dp)
    proj = jnp.dot(feat.T, pairw_ref[...], preferred_element_type=F32).astype(BF16).astype(F32)
    rowp_ref[...] = proj[:, 0:head].reshape(rowp_ref.shape)
    col_wide = proj[:, head : 2 * head]
    colp_ref[...] = col_wide
    w.landed(cot_in.at[pl.ds(0, n_seq - 1)], cot_recv)
    row_list = []
    for i in range(bins):
        row_list.append(jnp.sum(cot_ref[i].astype(F32) * col_wide, axis=0, keepdims=True))
    row_grad = jnp.concatenate(row_list, axis=0)
    col_grad = jnp.zeros((bins, head), F32)
    for p in range(n_seq):
        block = cot_in[p].astype(F32)
        for i in range(bins):
            col_grad = col_grad + block[i * bins : (i + 1) * bins] * rowp_ref[p, i : i + 1]
    grads[flat] = jnp.concatenate([row_grad, col_grad], axis=1).astype(BF16)
    grads_send, grads_recv = one(), one()

    def spread(k):
        peer = (flat + k + 1) % every
        w.send(
            grads.at[flat], grads.at[flat], grads_send, grads_recv, peer % n_seq, peer // n_seq
        )

    each(every - 1, spread)
    turned[dp] = feat
    saves = [
        save(turned.at[dp], turned_out.at[dp], 0),
        save(rowp_ref.at[me], rowp_out, 1),
        save(colp_ref, colp_out, 2),
    ]
    for y in range(mid):
        for d in range(1, n_dp):
            other = (dp + d) % n_dp
            ref = group(other, core, y)
            w.landed(ref, group_recv.at[other, core, y])
            w.send(ref, ref, beside_send, group_recv.at[other, core, y], w.sibling)
    for d in range(1, n_dp):
        other = (dp + d) % n_dp
        for y in range(mid):
            w.landed(group(other, 1 - core, y), group_recv.at[other, 1 - core, y])
        turned[other] = features(other)
        saves.append(save(turned.at[other], turned_out.at[other], 3 + d))
    w.landed(grads.at[pl.ds(0, every - 1)], grads_recv)
    saves.append(save(grads, grads_out, 3))

    w.landed(wkv_buf.at[pl.ds(0, n_seq - 1)], wkv_send)
    w.landed(wq_buf.at[pl.ds(0, n_seq - 2), pl.ds(0, share)], wq_send)
    w.landed(wq_buf.at[pl.ds(0, n_seq - 2), pl.ds(0, pieces - share)], x_send)
    w.landed(normed_ref.at[0], normed_send)
    w.landed(wq_buf.at[0], wq_beside)
    w.landed(wo_buf.at[0], wo_send)
    w.landed(kv_ref.at[0, pl.ds(0, chips - 1)], kv_sends[0])
    w.landed(kv_ref.at[0], kv_sends[1])
    w.landed(cot_in.at[pl.ds(0, n_seq - 1)], cot_send)
    for h in range(heads):
        w.landed(binned.at[h, pl.ds(0, chips - 1)], bin_send.at[h])
    w.landed(part_in, part_send)
    w.landed(pool_ref.at[0, 0, pl.ds(0, chips - 1)], own.send_sem.at[0])
    w.landed(pool_ref.at[0, 0], own.send_sem.at[1])
    w.landed(pool_ref.at[pl.ds(0, n_dp - 1), 0], across_send)
    w.landed(pool_ref.at[pl.ds(0, n_dp - 1), 0], beside_send)
    w.landed(grads.at[pl.ds(0, every - 1)], grads_send)
    for copy in saves:
        copy.wait()


def tail_kernel(rowp_ref, colp_ref, turned, grads, pair_ref, grow_ref, gcol_ref):
    for i in range(rowp_ref.shape[0]):
        pair_ref[i] = (rowp_ref[i : i + 1, :] * colp_ref[...]).astype(BF16)
    n_dp, width, count = turned.shape
    whole = merge_rows(grads[...], n_dp * count)
    total = jnp.zeros((width, whole.shape[1]), F32)
    for p in range(n_dp):
        part = whole[p * count : (p + 1) * count]
        total = total + jnp.dot(turned[p], part, preferred_element_type=F32)
    total = total.astype(BF16)
    channels = grow_ref.shape[1]
    grow_ref[...] = total[:, 0:channels]
    gcol_ref[...] = total[:, channels : 2 * channels]


def on_device(
    n_dp,
    n_seq,
    tokens,
    query_weight,
    key_weight,
    value_weight,
    output_weight,
    row_weight,
    col_weight,
    pair_cotangent,
):
    rows, width = tokens.shape[1:]
    shard, head = key_weight.shape
    heads_wide = query_weight.shape[1]
    half = heads_wide // 2
    bins, count, channels = pair_cotangent.shape[1:]
    third = shard // 3
    pieces, share = (6, 4) if shard % 96 == 0 else (3, 2)
    unit = shard // pieces
    chips = n_seq // 2
    mid = chips // LINE
    vmem = pl.BlockSpec(memory_space=pltpu.VMEM)
    hbm = pl.BlockSpec(memory_space=pltpu.HBM)
    dma = pltpu.SemaphoreType.DMA
    every = n_dp * n_seq
    heads = half // head
    grant = 60 * 2**20
    kept = pl.pallas_call(
        functools.partial(main_kernel, n_dp, n_seq, share),
        out_shape=(
            jax.ShapeDtypeStruct((bins, channels), F32),
            jax.ShapeDtypeStruct((count, channels), F32),
            jax.ShapeDtypeStruct((n_dp, width, count), BF16),
            jax.ShapeDtypeStruct((every, bins, 2 * channels), BF16),
        ),
        in_specs=[hbm] * 8,
        out_specs=(hbm,) * 4,
        scratch_shapes=[
            pltpu.VMEM((n_seq, bins, channels), F32),
            pltpu.VMEM((count, channels), F32),
            pltpu.VMEM((n_dp, width, count), BF16),
            pltpu.VMEM((every, bins, 2 * channels), BF16),
            pltpu.VMEM((rows, width), BF16),
            pltpu.VMEM((width, 2 * channels), BF16),
            pltpu.VMEM((bins, count, channels), BF16),
            pltpu.VMEM((n_seq, bins * bins, channels), BF16),
            pltpu.VMEM((n_seq, bins * bins, channels), BF16),
            pltpu.VMEM((2, 3, third, head), BF16),
            pltpu.VMEM((n_seq, 3, third, head), BF16),
            pltpu.VMEM((2, pieces, unit, half), BF16),
            pltpu.VMEM((n_seq, pieces, unit, half), BF16),
            pltpu.VMEM((2, 3, third, half), BF16),
            pltpu.VMEM((2, 3, third, half), BF16),
            pltpu.VMEM((2, rows, width), BF16),
            pltpu.VMEM((2, chips, 2 * rows, head), BF16),
            pltpu.VMEM((heads, chips, 2 * bins, head), BF16),
            pltpu.VMEM((2, shard, count), F32),
            pltpu.VMEM((shard, count), F32),
            pltpu.VMEM((n_dp, 2, chips, 3, third, count), BF16),
            dma((10,)),
            dma((3 + n_dp,)),
            dma((n_seq,)),
            dma((n_seq,)),
            dma((n_seq,)),
            dma((n_seq,)),
            dma((heads,)),
            dma((heads,)),
            dma((n_seq,)),
            dma((n_dp, 2, mid)),
            dma((20,)),
        ],
        compiler_params=pltpu.CompilerParams(
            collective_id=0, has_side_effects=True, vmem_limit_bytes=grant
        ),
    )(
        tokens[0],
        query_weight.reshape(pieces, unit, heads_wide),
        key_weight.reshape(3, third, head),
        value_weight.reshape(3, third, head),
        output_weight.reshape(3, third, heads_wide),
        row_weight,
        col_weight,
        pair_cotangent[0],
    )
    pair, grow, gcol = pl.pallas_call(
        tail_kernel,
        out_shape=(
            jax.ShapeDtypeStruct((bins, count, channels), BF16),
            jax.ShapeDtypeStruct((width, channels), BF16),
            jax.ShapeDtypeStruct((width, channels), BF16),
        ),
        in_specs=[vmem] * 4,
        out_specs=(vmem,) * 3,
        compiler_params=pltpu.CompilerParams(vmem_limit_bytes=grant),
    )(*kept)
    return (pair[None], grow, gcol)


def solution(mesh):
    placed = (
        P("dp", "seq", None),
        P("seq", None),
        P("seq", None),
        P("seq", None),
        P("seq", None),
        P(),
        P(),
        P("dp", "seq", None, None),
    )
    return jax.shard_map(
        functools.partial(on_device, mesh.shape["dp"], mesh.shape["seq"]),
        mesh=mesh,
        in_specs=placed,
        out_specs=(P("dp", "seq", None, None), P(), P()),
        check_vma=False,
    )
```

```python
import functools
import math

import jax
import jax.numpy as jnp
from jax import lax
from jax.experimental import pallas as pl
from jax.experimental.pallas import tpu as pltpu
from jax.sharding import PartitionSpec as P

POOL = 16
LINE = 4
ORDER = (1, LINE - 1, *range(2, LINE - 1))
F32 = jnp.float32
BF16 = jnp.bfloat16
MESH = pl.DeviceIdType.MESH
LAST = (((1,), (1,)), ((), ()))


def merge_rows(block, rows):
    if block.shape[1] % 16 == 0:
        return block.reshape(rows, block.shape[2])
    return block.astype(F32).reshape(rows, block.shape[2]).astype(block.dtype)


class Where:
    def __init__(self, n_dp, n_seq):
        self.n_dp, self.n_seq = n_dp, n_seq
        self.mid = n_seq // (LINE * 2)
        self.chips = n_seq // 2
        self.dp, self.me = lax.axis_index("dp"), lax.axis_index("seq")
        self.core = self.me % 2
        self.y = (self.me // 2) % self.mid
        self.z = self.me // (2 * self.mid)
        self.sibling = self.at(0, 0, True)

    def at(self, dz, dy, flip):
        z = (self.z + dz) % LINE
        y = (self.y + dy) % self.mid
        core = 1 - self.core if flip else self.core
        return (z * self.mid + y) * 2 + core

    def send(self, src, dst, send_sem, recv_sem, peer, dp=None):
        copy = pltpu.make_async_remote_copy(
            src_ref=src,
            dst_ref=dst,
            send_sem=send_sem,
            recv_sem=recv_sem,
            device_id=(self.dp if dp is None else dp, peer),
            device_id_type=MESH,
        )
        copy.start()

    def landed(self, ref, sem):
        pltpu.make_async_copy(ref, ref, sem).wait()


class Halves:
    def __init__(self, where, own, slot, send_sem, recv_sem):
        self.w, self.own, self.slot = where, own, slot
        self.send_sem, self.recv_sem = send_sem, recv_sem

    def give(self, peer, flip):
        w = self.w
        src = self.own(1 - w.core if flip else w.core)
        w.send(src, self.slot(w.me), self.send_sem, self.recv_sem.at[w.me], peer)

    def start_line(self):
        for dz in ORDER:
            for flip in (False, True):
                self.give(self.w.at(dz, 0, flip), flip)

    def start_mid(self):
        for dy in range(1, self.w.mid):
            for flip in (False, True):
                self.give(self.w.at(0, dy, flip), flip)

    def arrived(self, block):
        self.w.landed(self.slot(block), self.recv_sem.at[block])

    def pass_line(self):
        w = self.w
        for dz in ORDER:
            for flip in (False, True):
                block = w.at(dz, 0, flip)
                self.arrived(block)
                for dy in range(1, w.mid):
                    ref = self.slot(block)
                    w.send(ref, ref, self.send_sem, self.recv_sem.at[block], w.at(0, dy, False))

    def pass_mid(self):
        w = self.w
        for dz in (0, *ORDER):
            for dy in range(1, w.mid):
                for flip in (False, True):
                    block = w.at(dz, dy, flip)
                    self.arrived(block)


class Gather:
    def __init__(self, where, slot, send_sem, recv_sem):
        self.w, self.slot = where, slot
        self.send_sem, self.recv_sem = send_sem, recv_sem

    def push(self, block, peer, flip):
        ref = self.slot(block)
        sem = self.send_sem.at[1 if flip else 0]
        self.w.send(ref, ref, sem, self.recv_sem.at[block], peer)

    def arrived(self, block):
        self.w.landed(self.slot(block), self.recv_sem.at[block])

    def start(self):
        w = self.w
        for dz in ORDER:
            self.push(w.me, w.at(dz, 0, False), False)
        self.spread(0)

    def spread(self, dz):
        w = self.w
        block = w.at(dz, 0, False)
        for dy in range(1, w.mid):
            self.push(block, w.at(0, dy, False), False)
        self.push(block, w.sibling, True)

    def pass_line(self):
        for dz in ORDER:
            self.arrived(self.w.at(dz, 0, False))
            self.spread(dz)

    def pass_mid(self, dy):
        w = self.w
        for dz in (0, *ORDER):
            block = w.at(dz, dy, False)
            self.arrived(block)
            self.push(block, w.sibling, True)

    def complete(self):
        w = self.w
        for dz in (0, *ORDER):
            for dy in range(w.mid):
                self.arrived(w.at(dz, dy, True))


def each(total, act):
    def step(k, unused):
        act(k)
        return unused

    lax.fori_loop(0, total, step, 0)


def main_kernel(
    n_dp,
    n_seq,
    tok_hbm,
    wq_hbm,
    wk_hbm,
    wv_hbm,
    wo_hbm,
    roww_hbm,
    colw_hbm,
    cot_hbm,
    rowp_out,
    colp_out,
    turned,
    grads,
    rowp_ref,
    tok_ref,
    pairw_ref,
    cot_ref,
    pack,
    cot_in,
    wkv_own,
    wkv_buf,
    wq_own,
    wq_buf,
    wo_own,
    wo_buf,
    normed_ref,
    q_ref,
    kv_ref,
    binned,
    part_ref,
    part_in,
    pool_ref,
    load_sem,
    wkv_recv,
    wq_recv,
    kv_recv,
    bin_send,
    bin_recv,
    pool_recv,
    group_recv,
    sems,
):
    w = Where(n_dp, n_seq)
    dp, me, core, chips, mid = w.dp, w.me, w.core, w.chips, w.mid
    every = n_dp * n_seq
    flat = dp * n_seq + me
    head = wk_hbm.shape[2]
    half = wq_own.shape[3]
    heads = 2 * half // head
    rows, width = tok_ref.shape
    bins, count = cot_ref.shape[0:2]
    odd = dp % 2
    partner = dp + 1 - 2 * odd
    near = pl.multiple_of(odd * half, half)
    far = pl.multiple_of((1 - odd) * half, half)
    shard = width // n_seq
    sem = iter(range(sems.shape[0]))
    one = lambda: sems.at[next(sem)]

    sources = [
        (wk_hbm, wkv_own.at[0]),
        (wv_hbm, wkv_own.at[1]),
        (wq_hbm.at[:, :, pl.ds(near, half)], wq_own.at[0]),
        (wq_hbm.at[:, :, pl.ds(2 * half + near, half)], wq_own.at[1]),
        (tok_hbm, tok_ref),
        (wo_hbm.at[:, :, pl.ds(near, half)], wo_own.at[0, :, :, pl.ds(0, half)]),
        (wo_hbm.at[:, :, pl.ds(far, half)], wo_own.at[0, :, :, pl.ds(half, half)]),
        (wo_hbm.at[:, :, pl.ds(2 * half + near, half)], wo_own.at[1, :, :, pl.ds(0, half)]),
        (wo_hbm.at[:, :, pl.ds(2 * half + far, half)], wo_own.at[1, :, :, pl.ds(half, half)]),
        (cot_hbm, cot_ref),
        (roww_hbm, pairw_ref.at[:, pl.ds(0, head)]),
        (colw_hbm, pairw_ref.at[:, pl.ds(head, head)]),
    ]
    loads = [
        pltpu.make_async_copy(src, dst, load_sem.at[i]) for i, (src, dst) in enumerate(sources)
    ]
    for load in loads:
        load.start()

    barrier = pltpu.get_barrier_semaphore()

    def greet(k):
        peer = (flat + k + 1) % every
        pl.semaphore_signal(
            barrier, inc=1, device_id=(peer // n_seq, peer % n_seq), device_id_type=MESH
        )

    each(every - 1, greet)
    loads[4].wait()
    tok = tok_ref[...].astype(F32)
    normed_ref[0, core] = (
        tok * lax.rsqrt(jnp.mean(tok * tok, axis=1, keepdims=True) + 1e-06)
    ).astype(BF16)
    for load in loads[0:4]:
        load.wait()

    wkv_send, wq_send = one(), one()
    wkv = Halves(w, lambda c: wkv_own.at[c], lambda s: wkv_buf.at[s], wkv_send, wkv_recv)
    wq = Halves(w, lambda c: wq_own.at[c], lambda s: wq_buf.at[s], wq_send, wq_recv)

    def repack():
        loads[9].wait()
        squares = cot_ref[...].astype(F32)
        for p in range(n_seq):
            pack[p] = jnp.concatenate(
                [squares[i, p * bins : (p + 1) * bins] for i in range(bins)], axis=0
            ).astype(BF16)
        cot_in[me] = pack[me]

    pl.semaphore_wait(barrier, every - 1)
    wkv.start_line()
    wkv.start_mid()
    wkv.give(w.sibling, True)
    across_recv = one()
    mine = normed_ref.at[0, core]
    normed_sends = one(), one(), one()
    w.send(mine, normed_ref.at[1, core], normed_sends[0], across_recv, me, partner)
    normed_recv, beside_recv = one(), one()
    w.send(mine, mine, normed_sends[1], normed_recv, w.sibling)
    wq.start_line()
    wq.give(w.sibling, True)
    wkv_buf[me] = wkv_own[core]
    wq_buf[me] = wq_own[core]
    repack()
    wkv.pass_line()
    wq.start_mid()
    for load in loads[5:9]:
        load.wait()
    wo_send, wo_recv = one(), one()
    w.send(wo_own.at[1 - core], wo_buf.at[core], wo_send, wo_recv, w.sibling)
    wo_buf[core] = wo_own[core]
    w.landed(normed_ref.at[0, 1 - core], normed_recv)
    normed = normed_ref[0].reshape(2 * rows, width)
    wkv.pass_mid()
    wkv.arrived(w.sibling)

    def whole(buf):
        return merge_rows(
            buf[...].reshape(n_seq * buf.shape[1], buf.shape[2], buf.shape[3]), width
        )

    kv_ref[core, me // 2] = jnp.dot(
        normed, whole(wkv_buf), preferred_element_type=F32
    ).astype(BF16)
    kv_sends = (one(), one())

    class Sends:
        def __init__(self, pair):
            self.at = pair

    blocks = Gather(w, lambda s: kv_ref.at[s % 2, s // 2], Sends(kv_sends), kv_recv)
    blocks.start()
    wq.pass_line()
    blocks.pass_line()
    other = normed_ref.at[1, core]
    w.landed(other, across_recv)
    w.send(other, other, normed_sends[2], beside_recv, w.sibling)
    wq.pass_mid()
    wq.arrived(w.sibling)
    w.landed(normed_ref.at[1, 1 - core], beside_recv)
    wq_all = whole(wq_buf)
    q_ref[2] = jnp.dot(
        normed_ref[1].reshape(2 * rows, width), wq_all, preferred_element_type=F32
    ).astype(BF16)
    q_send, q_recv = one(), one()
    w.send(q_ref.at[2], q_ref.at[1], q_send, q_recv, me, partner)
    q_ref[0] = jnp.dot(normed, wq_all, preferred_element_type=F32).astype(BF16)
    for dy in range(1, mid):
        blocks.pass_mid(dy)
    blocks.complete()

    cot_send, cot_recv = one(), one()

    def turn(k):
        peer = (me + k + 1) % n_seq
        w.send(pack.at[peer], cot_in.at[me], cot_send, cot_recv, peer)

    each(n_seq - 1, turn)

    keys = kv_ref[0].reshape(n_seq * rows, head)
    values = kv_ref[1].reshape(n_seq * rows, head)
    factor = math.log2(math.e) / math.sqrt(head)
    chip_bins = 2 * bins
    per = half // head
    for h in range(heads):
        if h == per:
            w.landed(q_ref.at[1], q_recv)
        queries = q_ref[h // per, :, h % per * head : (h % per + 1) * head]
        scores = lax.dot_general(queries, keys, LAST, preferred_element_type=F32)
        top = jnp.max(scores, axis=1, keepdims=True)
        weights = jnp.exp2((scores - top) * factor)
        total = jnp.sum(weights, axis=1, keepdims=True)
        out = jnp.dot(weights.astype(BF16), values, preferred_element_type=F32) / total
        out = out.astype(BF16).astype(F32)
        binned[h, me // 2] = jnp.sum(out.reshape(chip_bins, POOL, head), axis=1).astype(BF16)
        ref = binned.at[h, me // 2]
        for dy in range(mid):
            for dz in (2, 1, 3, 0):
                if dz or dy:
                    w.send(ref, ref, bin_send.at[h], bin_recv.at[h], w.at(dz, dy, False))

    for load in loads[10:]:
        load.wait()
    w.landed(wo_buf.at[1 - core], wo_recv)
    wo = merge_rows(
        wo_buf[...].reshape(2 * wo_buf.shape[1], wo_buf.shape[2], 2 * half), 2 * shard
    )
    partial = jnp.zeros((2 * shard, count), F32)
    for h in range(heads):
        w.landed(binned.at[h, pl.ds(0, chips - 1)], bin_recv.at[h])
        partial = partial + lax.dot_general(
            wo[:, h * head : (h + 1) * head],
            binned[h].reshape(count, head),
            LAST,
            preferred_element_type=F32,
        )
    part_ref[0] = partial[0:shard]
    part_ref[1] = partial[shard : 2 * shard]
    part_send, part_recv = one(), one()
    w.send(part_ref.at[1 - core], part_in, part_send, part_recv, w.sibling)
    w.landed(part_in, part_recv)
    pooled = (part_ref[core] + part_in[...]) * (1.0 / POOL)
    spot = lambda s: ((s // 2) % mid) * LINE + s // (2 * mid)
    pool_ref[dp, core, spot(me)] = pooled.reshape(pool_ref.shape[3:]).astype(BF16)
    own = Gather(
        w, lambda s: pool_ref.at[dp, s % 2, spot(s)], Sends((one(), one())), pool_recv
    )
    own.start()
    across_send, beside_send = one(), one()

    def group(p, c, y):
        return pool_ref.at[p, c, pl.ds(y * LINE, LINE)]

    def across(y):
        for d in range(1, n_dp):
            ref = group(dp, core, y)
            w.send(ref, ref, across_send, group_recv.at[dp, core, y], me, (dp + d) % n_dp)

    own.pass_line()
    across(w.y)
    for dy in range(1, mid):
        own.pass_mid(dy)
        across((w.y + dy) % mid)
    own.complete()

    def features(p):
        stacked = jnp.concatenate(
            [
                pool_ref[p, c, y * LINE + z].astype(F32).reshape(shard, count)
                for z in range(LINE)
                for y in range(mid)
                for c in range(2)
            ],
            axis=0,
        )
        scale = lax.rsqrt(jnp.mean(stacked * stacked, axis=0, keepdims=True) + 1e-06)
        return (stacked * scale).astype(BF16)

    feat = features(dp)
    proj = jnp.dot(feat.T, pairw_ref[...], preferred_element_type=F32).astype(BF16).astype(F32)
    rowp_ref[...] = proj[:, 0:head].reshape(rowp_ref.shape)
    col_wide = proj[:, head : 2 * head]
    colp_out[...] = col_wide
    rowp_out[...] = rowp_ref[me]
    w.landed(cot_in.at[pl.ds(0, n_seq - 1)], cot_recv)
    row_list = []
    for i in range(bins):
        row_list.append(jnp.sum(cot_ref[i].astype(F32) * col_wide, axis=0, keepdims=True))
    row_grad = jnp.concatenate(row_list, axis=0)
    col_grad = jnp.zeros((bins, head), F32)
    for p in range(n_seq):
        block = cot_in[p].astype(F32)
        for i in range(bins):
            col_grad = col_grad + block[i * bins : (i + 1) * bins] * rowp_ref[p, i : i + 1]
    grads[flat] = jnp.concatenate([row_grad, col_grad], axis=1).astype(BF16)
    grads_send, grads_recv = one(), one()

    def spread(k):
        peer = (flat + k + 1) % every
        w.send(
            grads.at[flat], grads.at[flat], grads_send, grads_recv, peer % n_seq, peer // n_seq
        )

    each(every - 1, spread)
    turned[dp] = feat
    for y in range(mid):
        for d in range(1, n_dp):
            other = (dp + d) % n_dp
            ref = group(other, core, y)
            w.landed(ref, group_recv.at[other, core, y])
            w.send(ref, ref, beside_send, group_recv.at[other, core, y], w.sibling)
    for d in range(1, n_dp):
        other = (dp + d) % n_dp
        for y in range(mid):
            w.landed(group(other, 1 - core, y), group_recv.at[other, 1 - core, y])
        turned[other] = features(other)
    w.landed(grads.at[pl.ds(0, every - 1)], grads_recv)

    w.landed(wkv_buf.at[pl.ds(0, n_seq - 1)], wkv_send)
    w.landed(wq_buf.at[pl.ds(0, n_seq - 1)], wq_send)
    for normed_send in normed_sends:
        w.landed(normed_ref.at[0, 0], normed_send)
    w.landed(q_ref.at[1], q_send)
    w.landed(wo_buf.at[0], wo_send)
    w.landed(kv_ref.at[0, pl.ds(0, chips - 1)], kv_sends[0])
    w.landed(kv_ref.at[0], kv_sends[1])
    w.landed(cot_in.at[pl.ds(0, n_seq - 1)], cot_send)
    for h in range(heads):
        w.landed(binned.at[h, pl.ds(0, chips - 1)], bin_send.at[h])
    w.landed(part_in, part_send)
    w.landed(pool_ref.at[0, 0, pl.ds(0, chips - 1)], own.send_sem.at[0])
    w.landed(pool_ref.at[0, 0], own.send_sem.at[1])
    w.landed(pool_ref.at[pl.ds(0, n_dp - 1), 0], across_send)
    w.landed(pool_ref.at[pl.ds(0, n_dp - 1), 0], beside_send)
    w.landed(grads.at[pl.ds(0, every - 1)], grads_send)


def tail_kernel(rowp_ref, colp_ref, turned, grads, pair_ref, grow_ref, gcol_ref):
    for i in range(rowp_ref.shape[0]):
        pair_ref[i] = (rowp_ref[i : i + 1, :] * colp_ref[...]).astype(BF16)
    n_dp, width, count = turned.shape
    whole = merge_rows(grads[...], n_dp * count)
    total = jnp.zeros((width, whole.shape[1]), F32)
    for p in range(n_dp):
        part = whole[p * count : (p + 1) * count]
        total = total + jnp.dot(turned[p], part, preferred_element_type=F32)
    total = total.astype(BF16)
    channels = grow_ref.shape[1]
    grow_ref[...] = total[:, 0:channels]
    gcol_ref[...] = total[:, channels : 2 * channels]


def on_device(
    n_dp,
    n_seq,
    tokens,
    query_weight,
    key_weight,
    value_weight,
    output_weight,
    row_weight,
    col_weight,
    pair_cotangent,
):
    rows, width = tokens.shape[1:]
    shard, head = key_weight.shape
    heads_wide = query_weight.shape[1]
    half = heads_wide // 4
    bins, count, channels = pair_cotangent.shape[1:]
    third = shard // 3
    chips = n_seq // 2
    mid = chips // LINE
    vmem = pl.BlockSpec(memory_space=pltpu.VMEM)
    hbm = pl.BlockSpec(memory_space=pltpu.HBM)
    dma = pltpu.SemaphoreType.DMA
    every = n_dp * n_seq
    heads = 2 * half // head
    grant = 57 * 2**20 - 2 * every * bins * 2 * channels - 2 * n_dp * width * count - 4 * (bins + count) * channels
    tail_grant = 16 * 2**20 if n_dp * count <= 512 else 44 * 2**20
    kept = pl.pallas_call(
        functools.partial(main_kernel, n_dp, n_seq),
        out_shape=(
            pltpu.VMEM((bins, channels), F32),
            pltpu.VMEM((count, channels), F32),
            pltpu.VMEM((n_dp, width, count), BF16),
            pltpu.VMEM((every, bins, 2 * channels), BF16),
        ),
        in_specs=[hbm] * 8,
        out_specs=(vmem,) * 4,
        scratch_shapes=[
            pltpu.VMEM((n_seq, bins, channels), F32),
            pltpu.VMEM((rows, width), BF16),
            pltpu.VMEM((width, 2 * channels), BF16),
            pltpu.VMEM((bins, count, channels), BF16),
            pltpu.VMEM((n_seq, bins * bins, channels), BF16),
            pltpu.VMEM((n_seq, bins * bins, channels), BF16),
            pltpu.VMEM((2, 3, third, head), BF16),
            pltpu.VMEM((n_seq, 3, third, head), BF16),
            pltpu.VMEM((2, 3, third, half), BF16),
            pltpu.VMEM((n_seq, 3, third, half), BF16),
            pltpu.VMEM((2, 3, third, 2 * half), BF16),
            pltpu.VMEM((2, 3, third, 2 * half), BF16),
            pltpu.VMEM((2, 2, rows, width), BF16),
            pltpu.VMEM((3, 2 * rows, half), BF16),
            pltpu.VMEM((2, chips, 2 * rows, head), BF16),
            pltpu.VMEM((heads, chips, 2 * bins, head), BF16),
            pltpu.VMEM((2, shard, count), F32),
            pltpu.VMEM((shard, count), F32),
            pltpu.VMEM((n_dp, 2, chips, 3, third, count), BF16),
            dma((12,)),
            dma((n_seq,)),
            dma((n_seq,)),
            dma((n_seq,)),
            dma((heads,)),
            dma((heads,)),
            dma((n_seq,)),
            dma((n_dp, 2, mid)),
            dma((25,)),
        ],
        compiler_params=pltpu.CompilerParams(
            collective_id=0, has_side_effects=True, vmem_limit_bytes=grant
        ),
    )(
        tokens[0],
        query_weight.reshape(3, third, heads_wide),
        key_weight.reshape(3, third, head),
        value_weight.reshape(3, third, head),
        output_weight.reshape(3, third, heads_wide),
        row_weight,
        col_weight,
        pair_cotangent[0],
    )
    pair, grow, gcol = pl.pallas_call(
        tail_kernel,
        out_shape=(
            jax.ShapeDtypeStruct((bins, count, channels), BF16),
            jax.ShapeDtypeStruct((width, channels), BF16),
            jax.ShapeDtypeStruct((width, channels), BF16),
        ),
        in_specs=[vmem] * 4,
        out_specs=(vmem,) * 3,
        compiler_params=pltpu.CompilerParams(vmem_limit_bytes=tail_grant),
    )(*kept)
    return (pair[None], grow, gcol)


def solution(mesh):
    placed = (
        P("dp", "seq", None),
        P("seq", None),
        P("seq", None),
        P("seq", None),
        P("seq", None),
        P(),
        P(),
        P("dp", "seq", None, None),
    )
    return jax.shard_map(
        functools.partial(on_device, mesh.shape["dp"], mesh.shape["seq"]),
        mesh=mesh,
        in_specs=placed,
        out_specs=(P("dp", "seq", None, None), P(), P()),
        check_vma=False,
    )
```

```python
import functools
import math

import jax
import jax.numpy as jnp
from jax import lax
from jax.experimental import pallas as pl
from jax.experimental.pallas import tpu as pltpu
from jax.sharding import PartitionSpec as P

POOL = 16
LINE = 4
ORDER = (1, LINE - 1, *range(2, LINE - 1))
F32 = jnp.float32
BF16 = jnp.bfloat16
MESH = pl.DeviceIdType.MESH
LAST = (((1,), (1,)), ((), ()))


def merge_rows(block, rows):
    if block.shape[1] % 16 == 0:
        return block.reshape(rows, block.shape[2])
    return block.astype(F32).reshape(rows, block.shape[2]).astype(block.dtype)


class Where:
    def __init__(self, n_dp, n_seq):
        self.n_dp, self.n_seq = n_dp, n_seq
        self.mid = n_seq // (LINE * 2)
        self.chips = n_seq // 2
        self.dp, self.me = lax.axis_index("dp"), lax.axis_index("seq")
        self.core = self.me % 2
        self.y = (self.me // 2) % self.mid
        self.z = self.me // (2 * self.mid)
        self.sibling = self.at(0, 0, True)

    def at(self, dz, dy, flip):
        z = (self.z + dz) % LINE
        y = (self.y + dy) % self.mid
        core = 1 - self.core if flip else self.core
        return (z * self.mid + y) * 2 + core

    def send(self, src, dst, send_sem, recv_sem, peer, dp=None):
        copy = pltpu.make_async_remote_copy(
            src_ref=src,
            dst_ref=dst,
            send_sem=send_sem,
            recv_sem=recv_sem,
            device_id=(self.dp if dp is None else dp, peer),
            device_id_type=MESH,
        )
        copy.start()

    def landed(self, ref, sem):
        pltpu.make_async_copy(ref, ref, sem).wait()


class Halves:
    def __init__(self, where, own, slot, send_sem, recv_sem):
        self.w, self.own, self.slot = where, own, slot
        self.send_sem, self.recv_sem = send_sem, recv_sem

    def give(self, peer, flip):
        w = self.w
        src = self.own(1 - w.core if flip else w.core)
        w.send(src, self.slot(w.me), self.send_sem, self.recv_sem.at[w.me], peer)

    def start_line(self):
        for dz in ORDER:
            for flip in (False, True):
                self.give(self.w.at(dz, 0, flip), flip)

    def start_mid(self):
        for dy in range(1, self.w.mid):
            for flip in (False, True):
                self.give(self.w.at(0, dy, flip), flip)

    def arrived(self, block):
        self.w.landed(self.slot(block), self.recv_sem.at[block])

    def pass_line(self):
        w = self.w
        for dz in ORDER:
            for flip in (False, True):
                block = w.at(dz, 0, flip)
                self.arrived(block)
                for dy in range(1, w.mid):
                    ref = self.slot(block)
                    w.send(ref, ref, self.send_sem, self.recv_sem.at[block], w.at(0, dy, False))

    def pass_mid(self):
        w = self.w
        for dz in (0, *ORDER):
            for dy in range(1, w.mid):
                for flip in (False, True):
                    block = w.at(dz, dy, flip)
                    self.arrived(block)


class Gather:
    def __init__(self, where, slot, send_sem, recv_sem):
        self.w, self.slot = where, slot
        self.send_sem, self.recv_sem = send_sem, recv_sem

    def push(self, block, peer, flip):
        ref = self.slot(block)
        sem = self.send_sem.at[1 if flip else 0]
        self.w.send(ref, ref, sem, self.recv_sem.at[block], peer)

    def arrived(self, block):
        self.w.landed(self.slot(block), self.recv_sem.at[block])

    def start(self):
        w = self.w
        for dz in ORDER:
            self.push(w.me, w.at(dz, 0, False), False)
        self.spread(0)

    def spread(self, dz):
        w = self.w
        block = w.at(dz, 0, False)
        for dy in range(1, w.mid):
            self.push(block, w.at(0, dy, False), False)
        self.push(block, w.sibling, True)

    def pass_line(self):
        for dz in ORDER:
            self.arrived(self.w.at(dz, 0, False))
            self.spread(dz)

    def pass_mid(self, dy):
        w = self.w
        for dz in (0, *ORDER):
            block = w.at(dz, dy, False)
            self.arrived(block)
            self.push(block, w.sibling, True)

    def complete(self):
        w = self.w
        for dz in (0, *ORDER):
            for dy in range(w.mid):
                self.arrived(w.at(dz, dy, True))


def each(total, act):
    def step(k, unused):
        act(k)
        return unused

    lax.fori_loop(0, total, step, 0)


def main_kernel(
    n_dp,
    n_seq,
    tok_hbm,
    wq_hbm,
    wk_hbm,
    wv_hbm,
    wo_hbm,
    roww_hbm,
    colw_hbm,
    cot_hbm,
    rowp_out,
    colp_out,
    turned,
    grads,
    rowp_ref,
    tok_ref,
    pairw_ref,
    cot_ref,
    pack,
    cot_in,
    wkv_own,
    wkv_buf,
    wq_own,
    wq_buf,
    wo_own,
    wo_buf,
    normed_ref,
    q_ref,
    kv_ref,
    binned,
    part_ref,
    part_in,
    pool_ref,
    load_sem,
    wkv_recv,
    wq_recv,
    kv_recv,
    bin_send,
    bin_recv,
    pool_recv,
    group_recv,
    sems,
):
    w = Where(n_dp, n_seq)
    dp, me, core, chips, mid = w.dp, w.me, w.core, w.chips, w.mid
    every = n_dp * n_seq
    flat = dp * n_seq + me
    head = wk_hbm.shape[2]
    half = wq_own.shape[3]
    heads = 2 * half // head
    rows, width = tok_ref.shape
    bins, count = cot_ref.shape[0:2]
    odd = dp % 2
    partner = dp + 1 - 2 * odd
    near = pl.multiple_of(odd * half, half)
    far = pl.multiple_of((1 - odd) * half, half)
    shard = width // n_seq
    sem = iter(range(sems.shape[0]))
    one = lambda: sems.at[next(sem)]

    sources = [
        (wk_hbm, wkv_own.at[0]),
        (wv_hbm, wkv_own.at[1]),
        (wq_hbm.at[:, :, pl.ds(near, half)], wq_own.at[0]),
        (wq_hbm.at[:, :, pl.ds(2 * half + near, half)], wq_own.at[1]),
        (tok_hbm, tok_ref),
        (wo_hbm.at[:, :, pl.ds(near, half)], wo_own.at[0, :, :, pl.ds(0, half)]),
        (wo_hbm.at[:, :, pl.ds(far, half)], wo_own.at[0, :, :, pl.ds(half, half)]),
        (wo_hbm.at[:, :, pl.ds(2 * half + near, half)], wo_own.at[1, :, :, pl.ds(0, half)]),
        (wo_hbm.at[:, :, pl.ds(2 * half + far, half)], wo_own.at[1, :, :, pl.ds(half, half)]),
        (cot_hbm, cot_ref),
        (roww_hbm, pairw_ref.at[:, pl.ds(0, head)]),
        (colw_hbm, pairw_ref.at[:, pl.ds(head, head)]),
    ]
    loads = [
        pltpu.make_async_copy(src, dst, load_sem.at[i]) for i, (src, dst) in enumerate(sources)
    ]
    for load in loads:
        load.start()

    barrier = pltpu.get_barrier_semaphore()

    def greet(k):
        peer = (flat + k + 1) % every
        pl.semaphore_signal(
            barrier, inc=1, device_id=(peer // n_seq, peer % n_seq), device_id_type=MESH
        )

    each(every - 1, greet)
    loads[4].wait()
    tok = tok_ref[...].astype(F32)
    normed_ref[0, core] = (
        tok * lax.rsqrt(jnp.mean(tok * tok, axis=1, keepdims=True) + 1e-06)
    ).astype(BF16)
    for load in loads[0:4]:
        load.wait()

    wkv_send, wq_send = one(), one()
    wkv = Halves(w, lambda c: wkv_own.at[c], lambda s: wkv_buf.at[s], wkv_send, wkv_recv)
    wq = Halves(w, lambda c: wq_own.at[c], lambda s: wq_buf.at[s], wq_send, wq_recv)

    def repack():
        loads[9].wait()
        squares = cot_ref[...].astype(F32)
        for p in range(n_seq):
            pack[p] = jnp.concatenate(
                [squares[i, p * bins : (p + 1) * bins] for i in range(bins)], axis=0
            ).astype(BF16)
        cot_in[me] = pack[me]

    pl.semaphore_wait(barrier, every - 1)
    wkv.start_line()
    wkv.start_mid()
    wkv.give(w.sibling, True)
    across_recv = one()
    mine = normed_ref.at[0, core]
    normed_sends = one(), one(), one()
    w.send(mine, normed_ref.at[1, core], normed_sends[0], across_recv, me, partner)
    normed_recv, beside_recv = one(), one()
    w.send(mine, mine, normed_sends[1], normed_recv, w.sibling)
    wq.start_line()
    wq.give(w.sibling, True)
    wq.start_mid()
    wkv_buf[me] = wkv_own[core]
    wq_buf[me] = wq_own[core]
    repack()
    wkv.pass_line()
    for load in loads[5:9]:
        load.wait()
    wo_send, wo_recv = one(), one()
    w.send(wo_own.at[1 - core], wo_buf.at[core], wo_send, wo_recv, w.sibling)
    wo_buf[core] = wo_own[core]
    w.landed(normed_ref.at[0, 1 - core], normed_recv)
    normed = normed_ref[0].reshape(2 * rows, width)
    wkv.pass_mid()
    wkv.arrived(w.sibling)

    def whole(buf):
        return merge_rows(
            buf[...].reshape(n_seq * buf.shape[1], buf.shape[2], buf.shape[3]), width
        )

    cot_send, cot_recv = one(), one()

    def turn(k):
        peer = (me + k + 1) % n_seq
        w.send(pack.at[peer], cot_in.at[me], cot_send, cot_recv, peer)


    kv_ref[core, me // 2] = jnp.dot(
        normed, whole(wkv_buf), preferred_element_type=F32
    ).astype(BF16)
    kv_sends = (one(), one())

    class Sends:
        def __init__(self, pair):
            self.at = pair

    blocks = Gather(w, lambda s: kv_ref.at[s % 2, s // 2], Sends(kv_sends), kv_recv)
    blocks.start()
    wq.pass_line()
    blocks.pass_line()
    other = normed_ref.at[1, core]
    w.landed(other, across_recv)
    w.send(other, other, normed_sends[2], beside_recv, w.sibling)
    wq.pass_mid()
    wq.arrived(w.sibling)
    w.landed(normed_ref.at[1, 1 - core], beside_recv)
    wq_all = whole(wq_buf)
    q_ref[2] = jnp.dot(
        normed_ref[1].reshape(2 * rows, width), wq_all, preferred_element_type=F32
    ).astype(BF16)
    q_send, q_recv = one(), one()
    w.send(q_ref.at[2], q_ref.at[1], q_send, q_recv, me, partner)
    q_ref[0] = jnp.dot(normed, wq_all, preferred_element_type=F32).astype(BF16)
    for dy in range(1, mid):
        blocks.pass_mid(dy)
    blocks.complete()

    keys = kv_ref[0].reshape(n_seq * rows, head)
    values = kv_ref[1].reshape(n_seq * rows, head)
    factor = math.log2(math.e) / math.sqrt(head)
    chip_bins = 2 * bins
    per = half // head
    for h in range(heads):
        if h == per:
            w.landed(q_ref.at[1], q_recv)
        queries = q_ref[h // per, :, h % per * head : (h % per + 1) * head]
        scores = lax.dot_general(queries, keys, LAST, preferred_element_type=F32)
        top = jnp.max(scores, axis=1, keepdims=True)
        weights = jnp.exp2((scores - top) * factor)
        total = jnp.sum(weights, axis=1, keepdims=True)
        out = jnp.dot(weights.astype(BF16), values, preferred_element_type=F32) / total
        out = out.astype(BF16).astype(F32)
        binned[h, me // 2] = jnp.sum(out.reshape(chip_bins, POOL, head), axis=1).astype(BF16)
        ref = binned.at[h, me // 2]
        for dy in range(mid):
            for dz in (2, 1, 3, 0):
                if dz or dy:
                    w.send(ref, ref, bin_send.at[h], bin_recv.at[h], w.at(dz, dy, False))

    each(n_seq - 1, turn)
    for load in loads[10:]:
        load.wait()
    w.landed(wo_buf.at[1 - core], wo_recv)
    wo = merge_rows(
        wo_buf[...].reshape(2 * wo_buf.shape[1], wo_buf.shape[2], 2 * half), 2 * shard
    )
    partial = jnp.zeros((2 * shard, count), F32)
    for h in range(heads):
        w.landed(binned.at[h, pl.ds(0, chips - 1)], bin_recv.at[h])
        partial = partial + lax.dot_general(
            wo[:, h * head : (h + 1) * head],
            binned[h].reshape(count, head),
            LAST,
            preferred_element_type=F32,
        )
    part_ref[0] = partial[0:shard]
    part_ref[1] = partial[shard : 2 * shard]
    part_send, part_recv = one(), one()
    w.send(part_ref.at[1 - core], part_in, part_send, part_recv, w.sibling)
    w.landed(part_in, part_recv)
    pooled = (part_ref[core] + part_in[...]) * (1.0 / POOL)
    spot = lambda s: ((s // 2) % mid) * LINE + s // (2 * mid)
    pool_ref[dp, core, spot(me)] = pooled.reshape(pool_ref.shape[3:]).astype(BF16)
    own = Gather(
        w, lambda s: pool_ref.at[dp, s % 2, spot(s)], Sends((one(), one())), pool_recv
    )
    own.start()
    across_send, beside_send = one(), one()

    def group(p, c, y):
        return pool_ref.at[p, c, pl.ds(y * LINE, LINE)]

    def across(y):
        for d in range(1, n_dp):
            ref = group(dp, core, y)
            w.send(ref, ref, across_send, group_recv.at[dp, core, y], me, (dp + d) % n_dp)

    own.pass_line()
    across(w.y)
    for dy in range(1, mid):
        own.pass_mid(dy)
        across((w.y + dy) % mid)
    own.complete()

    def features(p):
        stacked = jnp.concatenate(
            [
                pool_ref[p, c, y * LINE + z].astype(F32).reshape(shard, count)
                for z in range(LINE)
                for y in range(mid)
                for c in range(2)
            ],
            axis=0,
        )
        scale = lax.rsqrt(jnp.mean(stacked * stacked, axis=0, keepdims=True) + 1e-06)
        return (stacked * scale).astype(BF16)

    feat = features(dp)
    proj = jnp.dot(feat.T, pairw_ref[...], preferred_element_type=F32).astype(BF16).astype(F32)
    rowp_ref[...] = proj[:, 0:head].reshape(rowp_ref.shape)
    col_wide = proj[:, head : 2 * head]
    colp_out[...] = col_wide
    rowp_out[...] = rowp_ref[me]
    w.landed(cot_in.at[pl.ds(0, n_seq - 1)], cot_recv)
    row_list = []
    for i in range(bins):
        row_list.append(jnp.sum(cot_ref[i].astype(F32) * col_wide, axis=0, keepdims=True))
    row_grad = jnp.concatenate(row_list, axis=0)
    col_grad = jnp.zeros((bins, head), F32)
    for p in range(n_seq):
        block = cot_in[p].astype(F32)
        for i in range(bins):
            col_grad = col_grad + block[i * bins : (i + 1) * bins] * rowp_ref[p, i : i + 1]
    grads[flat] = jnp.concatenate([row_grad, col_grad], axis=1).astype(BF16)
    grads_send, grads_recv = one(), one()

    def spread(k):
        peer = (flat + k + 1) % every
        w.send(
            grads.at[flat], grads.at[flat], grads_send, grads_recv, peer % n_seq, peer // n_seq
        )

    each(every - 1, spread)
    turned[dp] = feat
    for y in range(mid):
        for d in range(1, n_dp):
            other = (dp + d) % n_dp
            ref = group(other, core, y)
            w.landed(ref, group_recv.at[other, core, y])
            w.send(ref, ref, beside_send, group_recv.at[other, core, y], w.sibling)
    for d in range(1, n_dp):
        other = (dp + d) % n_dp
        for y in range(mid):
            w.landed(group(other, 1 - core, y), group_recv.at[other, 1 - core, y])
        turned[other] = features(other)
    w.landed(grads.at[pl.ds(0, every - 1)], grads_recv)

    w.landed(wkv_buf.at[pl.ds(0, n_seq - 1)], wkv_send)
    w.landed(wq_buf.at[pl.ds(0, n_seq - 1)], wq_send)
    for normed_send in normed_sends:
        w.landed(normed_ref.at[0, 0], normed_send)
    w.landed(q_ref.at[1], q_send)
    w.landed(wo_buf.at[0], wo_send)
    w.landed(kv_ref.at[0, pl.ds(0, chips - 1)], kv_sends[0])
    w.landed(kv_ref.at[0], kv_sends[1])
    w.landed(cot_in.at[pl.ds(0, n_seq - 1)], cot_send)
    for h in range(heads):
        w.landed(binned.at[h, pl.ds(0, chips - 1)], bin_send.at[h])
    w.landed(part_in, part_send)
    w.landed(pool_ref.at[0, 0, pl.ds(0, chips - 1)], own.send_sem.at[0])
    w.landed(pool_ref.at[0, 0], own.send_sem.at[1])
    w.landed(pool_ref.at[pl.ds(0, n_dp - 1), 0], across_send)
    w.landed(pool_ref.at[pl.ds(0, n_dp - 1), 0], beside_send)
    w.landed(grads.at[pl.ds(0, every - 1)], grads_send)


def tail_kernel(rowp_ref, colp_ref, turned, grads, pair_ref, grow_ref, gcol_ref):
    for i in range(rowp_ref.shape[0]):
        pair_ref[i] = (rowp_ref[i : i + 1, :] * colp_ref[...]).astype(BF16)
    n_dp, width, count = turned.shape
    whole = merge_rows(grads[...], n_dp * count)
    total = jnp.zeros((width, whole.shape[1]), F32)
    for p in range(n_dp):
        part = whole[p * count : (p + 1) * count]
        total = total + jnp.dot(turned[p], part, preferred_element_type=F32)
    total = total.astype(BF16)
    channels = grow_ref.shape[1]
    grow_ref[...] = total[:, 0:channels]
    gcol_ref[...] = total[:, channels : 2 * channels]


def on_device(
    n_dp,
    n_seq,
    tokens,
    query_weight,
    key_weight,
    value_weight,
    output_weight,
    row_weight,
    col_weight,
    pair_cotangent,
):
    rows, width = tokens.shape[1:]
    shard, head = key_weight.shape
    heads_wide = query_weight.shape[1]
    half = heads_wide // 4
    bins, count, channels = pair_cotangent.shape[1:]
    third = shard // 3
    chips = n_seq // 2
    mid = chips // LINE
    vmem = pl.BlockSpec(memory_space=pltpu.VMEM)
    hbm = pl.BlockSpec(memory_space=pltpu.HBM)
    dma = pltpu.SemaphoreType.DMA
    every = n_dp * n_seq
    heads = 2 * half // head
    grant = 57 * 2**20 - 2 * every * bins * 2 * channels - 2 * n_dp * width * count - 4 * (bins + count) * channels
    tail_grant = 16 * 2**20 if n_dp * count <= 512 else 44 * 2**20
    kept = pl.pallas_call(
        functools.partial(main_kernel, n_dp, n_seq),
        out_shape=(
            pltpu.VMEM((bins, channels), F32),
            pltpu.VMEM((count, channels), F32),
            pltpu.VMEM((n_dp, width, count), BF16),
            pltpu.VMEM((every, bins, 2 * channels), BF16),
        ),
        in_specs=[hbm] * 8,
        out_specs=(vmem,) * 4,
        scratch_shapes=[
            pltpu.VMEM((n_seq, bins, channels), F32),
            pltpu.VMEM((rows, width), BF16),
            pltpu.VMEM((width, 2 * channels), BF16),
            pltpu.VMEM((bins, count, channels), BF16),
            pltpu.VMEM((n_seq, bins * bins, channels), BF16),
            pltpu.VMEM((n_seq, bins * bins, channels), BF16),
            pltpu.VMEM((2, 3, third, head), BF16),
            pltpu.VMEM((n_seq, 3, third, head), BF16),
            pltpu.VMEM((2, 3, third, half), BF16),
            pltpu.VMEM((n_seq, 3, third, half), BF16),
            pltpu.VMEM((2, 3, third, 2 * half), BF16),
            pltpu.VMEM((2, 3, third, 2 * half), BF16),
            pltpu.VMEM((2, 2, rows, width), BF16),
            pltpu.VMEM((3, 2 * rows, half), BF16),
            pltpu.VMEM((2, chips, 2 * rows, head), BF16),
            pltpu.VMEM((heads, chips, 2 * bins, head), BF16),
            pltpu.VMEM((2, shard, count), F32),
            pltpu.VMEM((shard, count), F32),
            pltpu.VMEM((n_dp, 2, chips, 3, third, count), BF16),
            dma((12,)),
            dma((n_seq,)),
            dma((n_seq,)),
            dma((n_seq,)),
            dma((heads,)),
            dma((heads,)),
            dma((n_seq,)),
            dma((n_dp, 2, mid)),
            dma((25,)),
        ],
        compiler_params=pltpu.CompilerParams(
            collective_id=0, has_side_effects=True, vmem_limit_bytes=grant
        ),
    )(
        tokens[0],
        query_weight.reshape(3, third, heads_wide),
        key_weight.reshape(3, third, head),
        value_weight.reshape(3, third, head),
        output_weight.reshape(3, third, heads_wide),
        row_weight,
        col_weight,
        pair_cotangent[0],
    )
    pair, grow, gcol = pl.pallas_call(
        tail_kernel,
        out_shape=(
            jax.ShapeDtypeStruct((bins, count, channels), BF16),
            jax.ShapeDtypeStruct((width, channels), BF16),
            jax.ShapeDtypeStruct((width, channels), BF16),
        ),
        in_specs=[vmem] * 4,
        out_specs=(vmem,) * 3,
        compiler_params=pltpu.CompilerParams(vmem_limit_bytes=tail_grant),
    )(*kept)
    return (pair[None], grow, gcol)


def solution(mesh):
    placed = (
        P("dp", "seq", None),
        P("seq", None),
        P("seq", None),
        P("seq", None),
        P("seq", None),
        P(),
        P(),
        P("dp", "seq", None, None),
    )
    return jax.shard_map(
        functools.partial(on_device, mesh.shape["dp"], mesh.shape["seq"]),
        mesh=mesh,
        in_specs=placed,
        out_specs=(P("dp", "seq", None, None), P(), P()),
        check_vma=False,
    )
```

```python
import functools
import math

import jax
import jax.numpy as jnp
from jax import lax
from jax.experimental import pallas as pl
from jax.experimental.pallas import tpu as pltpu
from jax.sharding import PartitionSpec as P

POOL = 16
LINE = 4
TAIL = 3
ORDER = (1, LINE - 1, *range(2, LINE - 1))
F32 = jnp.float32
BF16 = jnp.bfloat16
MESH = pl.DeviceIdType.MESH
LAST = (((1,), (1,)), ((), ()))


def merge_rows(block, rows):
    if block.shape[1] % 16 == 0:
        return block.reshape(rows, block.shape[2])
    return block.astype(F32).reshape(rows, block.shape[2]).astype(block.dtype)


class Where:
    def __init__(self, n_dp, n_seq):
        self.n_dp, self.n_seq = n_dp, n_seq
        self.mid = n_seq // (LINE * 2)
        self.chips = n_seq // 2
        self.dp, self.me = lax.axis_index("dp"), lax.axis_index("seq")
        self.core = self.me % 2
        self.y = (self.me // 2) % self.mid
        self.z = self.me // (2 * self.mid)
        self.sibling = self.at(0, 0, True)

    def at(self, dz, dy, flip):
        z = (self.z + dz) % LINE
        y = (self.y + dy) % self.mid
        core = 1 - self.core if flip else self.core
        return (z * self.mid + y) * 2 + core

    def send(self, src, dst, send_sem, recv_sem, peer, dp=None):
        copy = pltpu.make_async_remote_copy(
            src_ref=src,
            dst_ref=dst,
            send_sem=send_sem,
            recv_sem=recv_sem,
            device_id=(self.dp if dp is None else dp, peer),
            device_id_type=MESH,
        )
        copy.start()

    def landed(self, ref, sem):
        pltpu.make_async_copy(ref, ref, sem).wait()


class Halves:
    def __init__(self, where, own, slot, send_sem, recv_sem):
        self.w, self.own, self.slot = where, own, slot
        self.send_sem, self.recv_sem = send_sem, recv_sem

    def give(self, peer, flip):
        w = self.w
        src = self.own(1 - w.core if flip else w.core)
        w.send(src, self.slot(w.me), self.send_sem, self.recv_sem.at[w.me], peer)

    def start_line(self):
        for dz in ORDER:
            for flip in (False, True):
                self.give(self.w.at(dz, 0, flip), flip)

    def start_mid(self):
        for dy in range(1, self.w.mid):
            for flip in (False, True):
                self.give(self.w.at(0, dy, flip), flip)

    def arrived(self, block):
        self.w.landed(self.slot(block), self.recv_sem.at[block])

    def pass_line(self):
        w = self.w
        for dz in ORDER:
            for flip in (False, True):
                block = w.at(dz, 0, flip)
                self.arrived(block)
                for dy in range(1, w.mid):
                    ref = self.slot(block)
                    w.send(ref, ref, self.send_sem, self.recv_sem.at[block], w.at(0, dy, False))

    def pass_mid(self):
        w = self.w
        for dz in (0, *ORDER):
            for dy in range(1, w.mid):
                for flip in (False, True):
                    block = w.at(dz, dy, flip)
                    self.arrived(block)


class Gather:
    def __init__(self, where, slot, send_sem, recv_sem):
        self.w, self.slot = where, slot
        self.send_sem, self.recv_sem = send_sem, recv_sem

    def push(self, block, peer, flip):
        ref = self.slot(block)
        sem = self.send_sem.at[1 if flip else 0]
        self.w.send(ref, ref, sem, self.recv_sem.at[block], peer)

    def arrived(self, block):
        self.w.landed(self.slot(block), self.recv_sem.at[block])

    def start(self):
        w = self.w
        for dz in ORDER:
            self.push(w.me, w.at(dz, 0, False), False)
        self.spread(0)

    def spread(self, dz):
        w = self.w
        block = w.at(dz, 0, False)
        for dy in range(1, w.mid):
            self.push(block, w.at(0, dy, False), False)
        self.push(block, w.sibling, True)

    def pass_line(self):
        for dz in ORDER:
            self.arrived(self.w.at(dz, 0, False))
            self.spread(dz)

    def pass_mid(self, dy):
        w = self.w
        for dz in (0, *ORDER):
            block = w.at(dz, dy, False)
            self.arrived(block)
            self.push(block, w.sibling, True)

    def complete(self):
        w = self.w
        for dz in (0, *ORDER):
            for dy in range(w.mid):
                self.arrived(w.at(dz, dy, True))


def each(total, act):
    def step(k, unused):
        act(k)
        return unused

    lax.fori_loop(0, total, step, 0)


def main_kernel(
    n_dp,
    n_seq,
    tok_hbm,
    wq_hbm,
    wk_hbm,
    wv_hbm,
    wo_hbm,
    roww_hbm,
    colw_hbm,
    cot_hbm,
    pair_out,
    turned,
    grads,
    rowp_ref,
    tok_ref,
    pairw_ref,
    cot_ref,
    pack,
    cot_in,
    wkv_own,
    wkv_buf,
    wq_own,
    wq_buf,
    wo_own,
    wo_buf,
    normed_ref,
    q_ref,
    kv_ref,
    binned,
    part_ref,
    part_in,
    pool_ref,
    load_sem,
    wkv_recv,
    wq_recv,
    kv_recv,
    bin_send,
    bin_recv,
    pool_recv,
    group_recv,
    sems,
):
    w = Where(n_dp, n_seq)
    dp, me, core, chips, mid = w.dp, w.me, w.core, w.chips, w.mid
    every = n_dp * n_seq
    flat = dp * n_seq + me
    head = wk_hbm.shape[2]
    half = wq_own.shape[3]
    heads = 2 * half // head
    rows, width = tok_ref.shape
    bins, count = cot_ref.shape[0:2]
    odd = dp % 2
    partner = dp + 1 - 2 * odd
    near = pl.multiple_of(odd * half, half)
    far = pl.multiple_of((1 - odd) * half, half)
    shard = width // n_seq
    sem = iter(range(sems.shape[0]))
    one = lambda: sems.at[next(sem)]

    sources = [
        (wk_hbm, wkv_own.at[0]),
        (wv_hbm, wkv_own.at[1]),
        (wq_hbm.at[:, :, pl.ds(near, half)], wq_own.at[0]),
        (wq_hbm.at[:, :, pl.ds(2 * half + near, half)], wq_own.at[1]),
        (tok_hbm, tok_ref),
        (wo_hbm.at[:, :, pl.ds(near, half)], wo_own.at[0, :, :, pl.ds(0, half)]),
        (wo_hbm.at[:, :, pl.ds(far, half)], wo_own.at[0, :, :, pl.ds(half, half)]),
        (wo_hbm.at[:, :, pl.ds(2 * half + near, half)], wo_own.at[1, :, :, pl.ds(0, half)]),
        (wo_hbm.at[:, :, pl.ds(2 * half + far, half)], wo_own.at[1, :, :, pl.ds(half, half)]),
        (cot_hbm, cot_ref),
        (roww_hbm, pairw_ref.at[:, pl.ds(0, head)]),
        (colw_hbm, pairw_ref.at[:, pl.ds(head, head)]),
    ]
    loads = [
        pltpu.make_async_copy(src, dst, load_sem.at[i]) for i, (src, dst) in enumerate(sources)
    ]
    for load in loads:
        load.start()

    barrier = pltpu.get_barrier_semaphore()

    def greet(peer, p):
        pl.semaphore_signal(barrier, inc=1, device_id=(p, peer), device_id_type=MESH)

    if n_dp > 2:

        def greet_next(k):
            peer = (flat + k + 1) % every
            greet(peer % n_seq, peer // n_seq)

        each(every - 1, greet_next)
        met = every - 1
    else:
        near_by = [w.sibling]
        for flip in (False, True):
            near_by += [w.at(dz, 0, flip) for dz in ORDER]
            near_by += [w.at(0, dy, flip) for dy in range(1, mid)]
        for peer in near_by:
            greet(peer, dp)
        for d in range(1, n_dp):
            greet(me, (dp + d) % n_dp)
        met = len(near_by) + n_dp - 1
    loads[4].wait()
    tok = tok_ref[...].astype(F32)
    normed_ref[0, core] = (
        tok * lax.rsqrt(jnp.mean(tok * tok, axis=1, keepdims=True) + 1e-06)
    ).astype(BF16)
    for load in loads[0:4]:
        load.wait()

    wkv_send, wq_send = one(), one()
    wkv = Halves(w, lambda c: wkv_own.at[c], lambda s: wkv_buf.at[s], wkv_send, wkv_recv)
    wq = Halves(w, lambda c: wq_own.at[c], lambda s: wq_buf.at[s], wq_send, wq_recv)

    def repack():
        loads[9].wait()
        squares = cot_ref[...].astype(F32)
        for p in range(n_seq):
            pack[p] = jnp.concatenate(
                [squares[i, p * bins : (p + 1) * bins] for i in range(bins)], axis=0
            ).astype(BF16)
        cot_in[me] = pack[me]

    pl.semaphore_wait(barrier, met)
    wkv.start_line()
    wkv.start_mid()
    wkv.give(w.sibling, True)
    across_recv = one()
    mine = normed_ref.at[0, core]
    normed_sends = one(), one(), one()
    w.send(mine, normed_ref.at[1, core], normed_sends[0], across_recv, me, partner)
    normed_recv, beside_recv = one(), one()
    w.send(mine, mine, normed_sends[1], normed_recv, w.sibling)
    wq.start_line()
    wq.give(w.sibling, True)
    wq.start_mid()
    wkv_buf[me] = wkv_own[core]
    wq_buf[me] = wq_own[core]
    repack()
    wkv.pass_line()
    for load in loads[5:9]:
        load.wait()
    wo_send, wo_recv = one(), one()
    w.send(wo_own.at[1 - core], wo_buf.at[core], wo_send, wo_recv, w.sibling)
    wo_buf[core] = wo_own[core]
    w.landed(normed_ref.at[0, 1 - core], normed_recv)
    normed = normed_ref[0].reshape(2 * rows, width)
    wkv.pass_mid()
    wkv.arrived(w.sibling)

    def whole(buf):
        return merge_rows(
            buf[...].reshape(n_seq * buf.shape[1], buf.shape[2], buf.shape[3]), width
        )

    cot_send, cot_recv = one(), one()

    def turn(k):
        peer = (me + k + 1) % n_seq
        w.send(pack.at[peer], cot_in.at[me], cot_send, cot_recv, peer)


    kv_ref[core, me // 2] = jnp.dot(
        normed, whole(wkv_buf), preferred_element_type=F32
    ).astype(BF16)
    kv_sends = (one(), one())

    class Sends:
        def __init__(self, pair):
            self.at = pair

    blocks = Gather(w, lambda s: kv_ref.at[s % 2, s // 2], Sends(kv_sends), kv_recv)
    blocks.start()
    wq.pass_line()
    blocks.pass_line()
    other = normed_ref.at[1, core]
    w.landed(other, across_recv)
    w.send(other, other, normed_sends[2], beside_recv, w.sibling)
    wq.pass_mid()
    wq.arrived(w.sibling)
    w.landed(normed_ref.at[1, 1 - core], beside_recv)
    wq_all = whole(wq_buf)
    q_ref[2] = jnp.dot(
        normed_ref[1].reshape(2 * rows, width), wq_all, preferred_element_type=F32
    ).astype(BF16)
    q_send, q_recv = one(), one()
    w.send(q_ref.at[2], q_ref.at[1], q_send, q_recv, me, partner)
    q_ref[0] = jnp.dot(normed, wq_all, preferred_element_type=F32).astype(BF16)
    for dy in range(1, mid):
        blocks.pass_mid(dy)
    blocks.complete()

    keys = kv_ref[0].reshape(n_seq * rows, head)
    values = kv_ref[1].reshape(n_seq * rows, head)
    factor = math.log2(math.e) / math.sqrt(head)
    chip_bins = 2 * bins
    per = half // head
    for h in range(heads):
        if h == per:
            w.landed(q_ref.at[1], q_recv)
        queries = q_ref[h // per, :, h % per * head : (h % per + 1) * head]
        scores = lax.dot_general(queries, keys, LAST, preferred_element_type=F32)
        top = jnp.max(scores, axis=1, keepdims=True)
        weights = jnp.exp2((scores - top) * factor)
        total = jnp.sum(weights, axis=1, keepdims=True)
        out = jnp.dot(weights.astype(BF16), values, preferred_element_type=F32) / total
        out = out.astype(BF16).astype(F32)
        binned[h, me // 2] = jnp.sum(out.reshape(chip_bins, POOL, head), axis=1).astype(BF16)
        ref = binned.at[h, me // 2]
        for dy in range(mid):
            for dz in (2, 1, 3, 0):
                if dz or dy:
                    w.send(ref, ref, bin_send.at[h], bin_recv.at[h], w.at(dz, dy, False))

    each(n_seq - 1, turn)
    for load in loads[10:]:
        load.wait()
    w.landed(wo_buf.at[1 - core], wo_recv)
    wo = merge_rows(
        wo_buf[...].reshape(2 * wo_buf.shape[1], wo_buf.shape[2], 2 * half), 2 * shard
    )
    partial = jnp.zeros((2 * shard, count), F32)
    for h in range(heads):
        w.landed(binned.at[h, pl.ds(0, chips - 1)], bin_recv.at[h])
        partial = partial + lax.dot_general(
            wo[:, h * head : (h + 1) * head],
            binned[h].reshape(count, head),
            LAST,
            preferred_element_type=F32,
        )
    part_ref[0] = partial[0:shard]
    part_ref[1] = partial[shard : 2 * shard]
    part_send, part_recv = one(), one()
    w.send(part_ref.at[1 - core], part_in, part_send, part_recv, w.sibling)
    w.landed(part_in, part_recv)
    pooled = (part_ref[core] + part_in[...]) * (1.0 / POOL)
    spot = lambda s: ((s // 2) % mid) * LINE + s // (2 * mid)
    pool_ref[dp, core, spot(me)] = pooled.reshape(pool_ref.shape[3:]).astype(BF16)
    own = Gather(
        w, lambda s: pool_ref.at[dp, s % 2, spot(s)], Sends((one(), one())), pool_recv
    )
    own.start()
    across_send, beside_send = one(), one()

    def group(p, c, y):
        return pool_ref.at[p, c, pl.ds(y * LINE, LINE)]

    def across(y):
        for d in range(1, n_dp):
            ref = group(dp, core, y)
            w.send(ref, ref, across_send, group_recv.at[dp, core, y], me, (dp + d) % n_dp)

    own.pass_line()
    across(w.y)
    for dy in range(1, mid):
        own.pass_mid(dy)
        across((w.y + dy) % mid)
    own.complete()

    def features(p):
        stacked = jnp.concatenate(
            [
                pool_ref[p, c, y * LINE + z].astype(F32).reshape(shard, count)
                for z in range(LINE)
                for y in range(mid)
                for c in range(2)
            ],
            axis=0,
        )
        scale = lax.rsqrt(jnp.mean(stacked * stacked, axis=0, keepdims=True) + 1e-06)
        return (stacked * scale).astype(BF16)

    feat = features(dp)
    proj = jnp.dot(feat.T, pairw_ref[...], preferred_element_type=F32).astype(BF16).astype(F32)
    rowp_ref[...] = proj[:, 0:head].reshape(rowp_ref.shape)
    col_wide = proj[:, head : 2 * head]
    w.landed(cot_in.at[pl.ds(0, n_seq - 1)], cot_recv)
    row_list = []
    for i in range(bins):
        row_list.append(jnp.sum(cot_ref[i].astype(F32) * col_wide, axis=0, keepdims=True))
    row_grad = jnp.concatenate(row_list, axis=0)
    col_grad = jnp.zeros((bins, head), F32)
    for p in range(n_seq):
        block = cot_in[p].astype(F32)
        for i in range(bins):
            col_grad = col_grad + block[i * bins : (i + 1) * bins] * rowp_ref[p, i : i + 1]
    grads[flat] = jnp.concatenate([row_grad, col_grad], axis=1).astype(BF16)
    grads_send, grads_recv = one(), one()

    def spread(k):
        peer = (flat + k + 1) % every
        w.send(
            grads.at[flat], grads.at[flat], grads_send, grads_recv, peer % n_seq, peer // n_seq
        )

    each(every - 1, spread)
    turned[dp] = feat
    for i in range(bins):
        pair_out[i] = (rowp_ref[me, i : i + 1] * col_wide).astype(BF16)
    for y in range(mid):
        for d in range(1, n_dp):
            other = (dp + d) % n_dp
            ref = group(other, core, y)
            w.landed(ref, group_recv.at[other, core, y])
            w.send(ref, ref, beside_send, group_recv.at[other, core, y], w.sibling)
    for d in range(1, n_dp):
        other = (dp + d) % n_dp
        for y in range(mid):
            w.landed(group(other, 1 - core, y), group_recv.at[other, 1 - core, y])
        turned[other] = features(other)
    w.landed(grads.at[pl.ds(0, every - 1)], grads_recv)

    w.landed(wkv_buf.at[pl.ds(0, n_seq - 1)], wkv_send)
    w.landed(wq_buf.at[pl.ds(0, n_seq - 1)], wq_send)
    for normed_send in normed_sends:
        w.landed(normed_ref.at[0, 0], normed_send)
    w.landed(q_ref.at[1], q_send)
    w.landed(wo_buf.at[0], wo_send)
    w.landed(kv_ref.at[0, pl.ds(0, chips - 1)], kv_sends[0])
    w.landed(kv_ref.at[0], kv_sends[1])
    w.landed(cot_in.at[pl.ds(0, n_seq - 1)], cot_send)
    for h in range(heads):
        w.landed(binned.at[h, pl.ds(0, chips - 1)], bin_send.at[h])
    w.landed(part_in, part_send)
    w.landed(pool_ref.at[0, 0, pl.ds(0, chips - 1)], own.send_sem.at[0])
    w.landed(pool_ref.at[0, 0], own.send_sem.at[1])
    w.landed(pool_ref.at[pl.ds(0, n_dp - 1), 0], across_send)
    w.landed(pool_ref.at[pl.ds(0, n_dp - 1), 0], beside_send)
    w.landed(grads.at[pl.ds(0, every - 1)], grads_send)


def tail_kernel(pair_ref, turned, grads, pair_hbm, grow_hbm, gcol_hbm, out_ref, sems):
    pair_copy = pltpu.make_async_copy(pair_ref, pair_hbm, sems.at[0])
    pair_copy.start()
    n_dp, width, count = turned.shape
    channels = grow_hbm.shape[1]
    whole = merge_rows(grads[...], n_dp * count)
    step = width // TAIL
    copies = [pair_copy]
    for k in range(TAIL):
        total = jnp.zeros((step, whole.shape[1]), F32)
        for p in range(n_dp):
            total = total + jnp.dot(
                turned[p, k * step : (k + 1) * step],
                whole[p * count : (p + 1) * count],
                preferred_element_type=F32,
            )
        total = total.astype(BF16)
        for c, target in enumerate((grow_hbm, gcol_hbm)):
            ref = out_ref.at[c, pl.ds(k * step, step)]
            ref[...] = total[:, c * channels : (c + 1) * channels]
            copy = pltpu.make_async_copy(
                ref, target.at[pl.ds(k * step, step)], sems.at[1 + 2 * k + c]
            )
            copy.start()
            copies.append(copy)
    for copy in copies:
        copy.wait()


def on_device(
    n_dp,
    n_seq,
    tokens,
    query_weight,
    key_weight,
    value_weight,
    output_weight,
    row_weight,
    col_weight,
    pair_cotangent,
):
    rows, width = tokens.shape[1:]
    shard, head = key_weight.shape
    heads_wide = query_weight.shape[1]
    half = heads_wide // 4
    bins, count, channels = pair_cotangent.shape[1:]
    third = shard // 3
    chips = n_seq // 2
    mid = chips // LINE
    vmem = pl.BlockSpec(memory_space=pltpu.VMEM)
    hbm = pl.BlockSpec(memory_space=pltpu.HBM)
    dma = pltpu.SemaphoreType.DMA
    every = n_dp * n_seq
    heads = 2 * half // head
    results = every * bins * 2 * channels + n_dp * width * count + bins * count * channels
    grant = 57 * 2**20 - 2 * results
    tail_grant = 16 * 2**20 if n_dp * count <= 512 else 44 * 2**20
    kept = pl.pallas_call(
        functools.partial(main_kernel, n_dp, n_seq),
        out_shape=(
            pltpu.VMEM((bins, count, channels), BF16),
            pltpu.VMEM((n_dp, width, count), BF16),
            pltpu.VMEM((every, bins, 2 * channels), BF16),
        ),
        in_specs=[hbm] * 8,
        out_specs=(vmem,) * 3,
        scratch_shapes=[
            pltpu.VMEM((n_seq, bins, channels), F32),
            pltpu.VMEM((rows, width), BF16),
            pltpu.VMEM((width, 2 * channels), BF16),
            pltpu.VMEM((bins, count, channels), BF16),
            pltpu.VMEM((n_seq, bins * bins, channels), BF16),
            pltpu.VMEM((n_seq, bins * bins, channels), BF16),
            pltpu.VMEM((2, 3, third, head), BF16),
            pltpu.VMEM((n_seq, 3, third, head), BF16),
            pltpu.VMEM((2, 3, third, half), BF16),
            pltpu.VMEM((n_seq, 3, third, half), BF16),
            pltpu.VMEM((2, 3, third, 2 * half), BF16),
            pltpu.VMEM((2, 3, third, 2 * half), BF16),
            pltpu.VMEM((2, 2, rows, width), BF16),
            pltpu.VMEM((3, 2 * rows, half), BF16),
            pltpu.VMEM((2, chips, 2 * rows, head), BF16),
            pltpu.VMEM((heads, chips, 2 * bins, head), BF16),
            pltpu.VMEM((2, shard, count), F32),
            pltpu.VMEM((shard, count), F32),
            pltpu.VMEM((n_dp, 2, chips, 3, third, count), BF16),
            dma((12,)),
            dma((n_seq,)),
            dma((n_seq,)),
            dma((n_seq,)),
            dma((heads,)),
            dma((heads,)),
            dma((n_seq,)),
            dma((n_dp, 2, mid)),
            dma((25,)),
        ],
        compiler_params=pltpu.CompilerParams(
            collective_id=0, has_side_effects=True, vmem_limit_bytes=grant
        ),
    )(
        tokens[0],
        query_weight.reshape(3, third, heads_wide),
        key_weight.reshape(3, third, head),
        value_weight.reshape(3, third, head),
        output_weight.reshape(3, third, heads_wide),
        row_weight,
        col_weight,
        pair_cotangent[0],
    )
    pair, grow, gcol = pl.pallas_call(
        tail_kernel,
        out_shape=(
            jax.ShapeDtypeStruct((bins, count, channels), BF16),
            jax.ShapeDtypeStruct((width, channels), BF16),
            jax.ShapeDtypeStruct((width, channels), BF16),
        ),
        in_specs=[vmem] * 3,
        out_specs=(hbm,) * 3,
        scratch_shapes=[pltpu.VMEM((2, width, channels), BF16), dma((1 + 2 * TAIL,))],
        compiler_params=pltpu.CompilerParams(vmem_limit_bytes=tail_grant),
    )(*kept)
    return (pair[None], grow, gcol)


def solution(mesh):
    placed = (
        P("dp", "seq", None),
        P("seq", None),
        P("seq", None),
        P("seq", None),
        P("seq", None),
        P(),
        P(),
        P("dp", "seq", None, None),
    )
    return jax.shard_map(
        functools.partial(on_device, mesh.shape["dp"], mesh.shape["seq"]),
        mesh=mesh,
        in_specs=placed,
        out_specs=(P("dp", "seq", None, None), P(), P()),
        check_vma=False,
    )
```

```python
import functools
import math

import jax
import jax.numpy as jnp
from jax import lax
from jax.experimental import pallas as pl
from jax.experimental.pallas import tpu as pltpu
from jax.sharding import PartitionSpec as P

POOL = 16
LINE = 4
TAIL = 3
ORDER = (1, LINE - 1, *range(2, LINE - 1))
F32 = jnp.float32
BF16 = jnp.bfloat16
MESH = pl.DeviceIdType.MESH
LAST = (((1,), (1,)), ((), ()))


def merge_rows(block, rows):
    if block.shape[1] % 16 == 0:
        return block.reshape(rows, block.shape[2])
    return block.astype(F32).reshape(rows, block.shape[2]).astype(block.dtype)


class Where:
    def __init__(self, n_dp, n_seq):
        self.n_dp, self.n_seq = n_dp, n_seq
        self.mid = n_seq // (LINE * 2)
        self.chips = n_seq // 2
        self.dp, self.me = lax.axis_index("dp"), lax.axis_index("seq")
        self.core = self.me % 2
        self.y = (self.me // 2) % self.mid
        self.z = self.me // (2 * self.mid)
        self.sibling = self.at(0, 0, True)

    def at(self, dz, dy, flip):
        z = (self.z + dz) % LINE
        y = (self.y + dy) % self.mid
        core = 1 - self.core if flip else self.core
        return (z * self.mid + y) * 2 + core

    def send(self, src, dst, send_sem, recv_sem, peer, dp=None):
        copy = pltpu.make_async_remote_copy(
            src_ref=src,
            dst_ref=dst,
            send_sem=send_sem,
            recv_sem=recv_sem,
            device_id=(self.dp if dp is None else dp, peer),
            device_id_type=MESH,
        )
        copy.start()

    def landed(self, ref, sem):
        pltpu.make_async_copy(ref, ref, sem).wait()


class Halves:
    def __init__(self, where, own, slot, send_sem, recv_sem):
        self.w, self.own, self.slot = where, own, slot
        self.send_sem, self.recv_sem = send_sem, recv_sem

    def give(self, peer, flip):
        w = self.w
        src = self.own(1 - w.core if flip else w.core)
        w.send(src, self.slot(w.me), self.send_sem, self.recv_sem.at[w.me], peer)

    def start_line(self):
        for dz in ORDER:
            for flip in (False, True):
                self.give(self.w.at(dz, 0, flip), flip)

    def start_mid(self):
        for dy in range(1, self.w.mid):
            for flip in (False, True):
                self.give(self.w.at(0, dy, flip), flip)

    def arrived(self, block):
        self.w.landed(self.slot(block), self.recv_sem.at[block])

    def pass_line(self):
        w = self.w
        for dz in ORDER:
            for flip in (False, True):
                block = w.at(dz, 0, flip)
                self.arrived(block)
                for dy in range(1, w.mid):
                    ref = self.slot(block)
                    w.send(ref, ref, self.send_sem, self.recv_sem.at[block], w.at(0, dy, False))

    def pass_mid(self):
        w = self.w
        for dz in (0, *ORDER):
            for dy in range(1, w.mid):
                for flip in (False, True):
                    block = w.at(dz, dy, flip)
                    self.arrived(block)


class Gather:
    def __init__(self, where, slot, send_sem, recv_sem):
        self.w, self.slot = where, slot
        self.send_sem, self.recv_sem = send_sem, recv_sem

    def push(self, block, peer, flip):
        ref = self.slot(block)
        sem = self.send_sem.at[1 if flip else 0]
        self.w.send(ref, ref, sem, self.recv_sem.at[block], peer)

    def arrived(self, block):
        self.w.landed(self.slot(block), self.recv_sem.at[block])

    def start(self):
        w = self.w
        for dz in ORDER:
            self.push(w.me, w.at(dz, 0, False), False)
        self.spread(0)

    def spread(self, dz):
        w = self.w
        block = w.at(dz, 0, False)
        for dy in range(1, w.mid):
            self.push(block, w.at(0, dy, False), False)
        self.push(block, w.sibling, True)

    def pass_line(self):
        for dz in ORDER:
            self.arrived(self.w.at(dz, 0, False))
            self.spread(dz)

    def pass_mid(self, dy):
        w = self.w
        for dz in (0, *ORDER):
            block = w.at(dz, dy, False)
            self.arrived(block)
            self.push(block, w.sibling, True)

    def complete(self):
        w = self.w
        for dz in (0, *ORDER):
            for dy in range(w.mid):
                self.arrived(w.at(dz, dy, True))


def each(total, act):
    def step(k, unused):
        act(k)
        return unused

    lax.fori_loop(0, total, step, 0)


def main_kernel(
    n_dp,
    n_seq,
    tok_hbm,
    wq_hbm,
    wk_hbm,
    wv_hbm,
    wo_hbm,
    roww_hbm,
    colw_hbm,
    cot_hbm,
    pair_out,
    turned,
    grads,
    rowp_ref,
    tok_ref,
    pairw_ref,
    cot_ref,
    pack,
    cot_in,
    wkv_own,
    wkv_buf,
    wq_own,
    wq_buf,
    wo_own,
    wo_buf,
    normed_ref,
    q_ref,
    kv_ref,
    binned,
    part_ref,
    part_in,
    pool_ref,
    load_sem,
    wkv_recv,
    wq_recv,
    kv_recv,
    bin_send,
    bin_recv,
    pool_recv,
    group_recv,
    sems,
):
    w = Where(n_dp, n_seq)
    dp, me, core, chips, mid = w.dp, w.me, w.core, w.chips, w.mid
    every = n_dp * n_seq
    flat = dp * n_seq + me
    head = wk_hbm.shape[2]
    half = wq_own.shape[3]
    heads = 2 * half // head
    rows, width = tok_ref.shape
    bins, count = cot_ref.shape[0:2]
    odd = dp % 2
    partner = dp + 1 - 2 * odd
    near = pl.multiple_of(odd * half, half)
    far = pl.multiple_of((1 - odd) * half, half)
    shard = width // n_seq
    sem = iter(range(sems.shape[0]))
    one = lambda: sems.at[next(sem)]

    sources = [
        (wk_hbm, wkv_own.at[0]),
        (wv_hbm, wkv_own.at[1]),
        (wq_hbm.at[:, :, pl.ds(near, half)], wq_own.at[0]),
        (wq_hbm.at[:, :, pl.ds(2 * half + near, half)], wq_own.at[1]),
        (tok_hbm, tok_ref),
        (wo_hbm.at[:, :, pl.ds(near, half)], wo_own.at[0, :, :, pl.ds(0, half)]),
        (wo_hbm.at[:, :, pl.ds(far, half)], wo_own.at[0, :, :, pl.ds(half, half)]),
        (wo_hbm.at[:, :, pl.ds(2 * half + near, half)], wo_own.at[1, :, :, pl.ds(0, half)]),
        (wo_hbm.at[:, :, pl.ds(2 * half + far, half)], wo_own.at[1, :, :, pl.ds(half, half)]),
        (cot_hbm, cot_ref),
        (roww_hbm, pairw_ref.at[:, pl.ds(0, head)]),
        (colw_hbm, pairw_ref.at[:, pl.ds(head, head)]),
    ]
    loads = [
        pltpu.make_async_copy(src, dst, load_sem.at[i]) for i, (src, dst) in enumerate(sources)
    ]
    for load in loads:
        load.start()

    barrier = pltpu.get_barrier_semaphore()

    def greet(peer, p):
        pl.semaphore_signal(barrier, inc=1, device_id=(p, peer), device_id_type=MESH)

    if n_dp > 2:

        def greet_next(k):
            peer = (flat + k + 1) % every
            greet(peer % n_seq, peer // n_seq)

        each(every - 1, greet_next)
        met = every - 1
    else:
        near_by = [w.sibling]
        for flip in (False, True):
            near_by += [w.at(dz, 0, flip) for dz in ORDER]
            near_by += [w.at(0, dy, flip) for dy in range(1, mid)]
        for peer in near_by:
            greet(peer, dp)
        for d in range(1, n_dp):
            greet(me, (dp + d) % n_dp)
        met = len(near_by) + n_dp - 1
    loads[4].wait()
    tok = tok_ref[...].astype(F32)
    normed_ref[0, core] = (
        tok * lax.rsqrt(jnp.mean(tok * tok, axis=1, keepdims=True) + 1e-06)
    ).astype(BF16)
    for load in loads[0:4]:
        load.wait()

    wkv_send, wq_send = one(), one()
    wkv = Halves(w, lambda c: wkv_own.at[c], lambda s: wkv_buf.at[s], wkv_send, wkv_recv)
    wq = Halves(w, lambda c: wq_own.at[c], lambda s: wq_buf.at[s], wq_send, wq_recv)

    def repack():
        loads[9].wait()
        squares = cot_ref[...].astype(F32)
        for p in range(n_seq):
            pack[p] = jnp.concatenate(
                [squares[i, p * bins : (p + 1) * bins] for i in range(bins)], axis=0
            ).astype(BF16)
        cot_in[me] = pack[me]

    pl.semaphore_wait(barrier, met)
    across_recv = one()
    mine = normed_ref.at[0, core]
    normed_sends = one(), one(), one()
    w.send(mine, normed_ref.at[1, core], normed_sends[0], across_recv, me, partner)
    normed_recv, beside_recv = one(), one()
    w.send(mine, mine, normed_sends[1], normed_recv, w.sibling)
    wkv.start_line()
    wkv.start_mid()
    wkv.give(w.sibling, True)
    wq.start_line()
    wq.give(w.sibling, True)
    wq.start_mid()
    wkv_buf[me] = wkv_own[core]
    wq_buf[me] = wq_own[core]
    repack()
    wkv.pass_line()
    for load in loads[5:9]:
        load.wait()
    wo_send, wo_recv = one(), one()
    w.send(wo_own.at[1 - core], wo_buf.at[core], wo_send, wo_recv, w.sibling)
    wo_buf[core] = wo_own[core]
    w.landed(normed_ref.at[0, 1 - core], normed_recv)
    normed = normed_ref[0].reshape(2 * rows, width)
    wkv.pass_mid()
    wkv.arrived(w.sibling)

    def whole(buf):
        return merge_rows(
            buf[...].reshape(n_seq * buf.shape[1], buf.shape[2], buf.shape[3]), width
        )

    cot_send, cot_recv = one(), one()

    def turn(k):
        peer = (me + k + 1) % n_seq
        w.send(pack.at[peer], cot_in.at[me], cot_send, cot_recv, peer)


    kv_ref[core, me // 2] = jnp.dot(
        normed, whole(wkv_buf), preferred_element_type=F32
    ).astype(BF16)
    kv_sends = (one(), one())

    class Sends:
        def __init__(self, pair):
            self.at = pair

    blocks = Gather(w, lambda s: kv_ref.at[s % 2, s // 2], Sends(kv_sends), kv_recv)
    blocks.start()
    wq.pass_line()
    blocks.pass_line()
    other = normed_ref.at[1, core]
    w.landed(other, across_recv)
    w.send(other, other, normed_sends[2], beside_recv, w.sibling)
    wq.pass_mid()
    wq.arrived(w.sibling)
    w.landed(normed_ref.at[1, 1 - core], beside_recv)
    wq_all = whole(wq_buf)
    q_ref[2] = jnp.dot(
        normed_ref[1].reshape(2 * rows, width), wq_all, preferred_element_type=F32
    ).astype(BF16)
    q_send, q_recv = one(), one()
    w.send(q_ref.at[2], q_ref.at[1], q_send, q_recv, me, partner)
    q_ref[0] = jnp.dot(normed, wq_all, preferred_element_type=F32).astype(BF16)
    for dy in range(1, mid):
        blocks.pass_mid(dy)
    blocks.complete()

    keys = kv_ref[0].reshape(n_seq * rows, head)
    values = kv_ref[1].reshape(n_seq * rows, head)
    factor = math.log2(math.e) / math.sqrt(head)
    chip_bins = 2 * bins
    per = half // head
    for h in range(heads):
        if h == per:
            w.landed(q_ref.at[1], q_recv)
        queries = q_ref[h // per, :, h % per * head : (h % per + 1) * head]
        scores = lax.dot_general(queries, keys, LAST, preferred_element_type=F32)
        top = jnp.max(scores, axis=1, keepdims=True)
        weights = jnp.exp2((scores - top) * factor)
        total = jnp.sum(weights, axis=1, keepdims=True)
        out = jnp.dot(weights.astype(BF16), values, preferred_element_type=F32) / total
        out = out.astype(BF16).astype(F32)
        binned[h, me // 2] = jnp.sum(out.reshape(chip_bins, POOL, head), axis=1).astype(BF16)
        ref = binned.at[h, me // 2]
        for dy in range(mid):
            for dz in (2, 1, 3, 0):
                if dz or dy:
                    w.send(ref, ref, bin_send.at[h], bin_recv.at[h], w.at(dz, dy, False))

    each(n_seq - 1, turn)
    for load in loads[10:]:
        load.wait()
    w.landed(wo_buf.at[1 - core], wo_recv)
    wo = merge_rows(
        wo_buf[...].reshape(2 * wo_buf.shape[1], wo_buf.shape[2], 2 * half), 2 * shard
    )
    partial = jnp.zeros((2 * shard, count), F32)
    for h in range(heads):
        w.landed(binned.at[h, pl.ds(0, chips - 1)], bin_recv.at[h])
        partial = partial + lax.dot_general(
            wo[:, h * head : (h + 1) * head],
            binned[h].reshape(count, head),
            LAST,
            preferred_element_type=F32,
        )
    part_ref[0] = partial[0:shard]
    part_ref[1] = partial[shard : 2 * shard]
    part_send, part_recv = one(), one()
    w.send(part_ref.at[1 - core], part_in, part_send, part_recv, w.sibling)
    w.landed(part_in, part_recv)
    pooled = (part_ref[core] + part_in[...]) * (1.0 / POOL)
    spot = lambda s: ((s // 2) % mid) * LINE + s // (2 * mid)
    pool_ref[dp, core, spot(me)] = pooled.reshape(pool_ref.shape[3:]).astype(BF16)
    own = Gather(
        w, lambda s: pool_ref.at[dp, s % 2, spot(s)], Sends((one(), one())), pool_recv
    )
    own.start()
    across_send, beside_send = one(), one()

    def group(p, c, y):
        return pool_ref.at[p, c, pl.ds(y * LINE, LINE)]

    def across(y):
        for d in range(1, n_dp):
            ref = group(dp, core, y)
            w.send(ref, ref, across_send, group_recv.at[dp, core, y], me, (dp + d) % n_dp)

    own.pass_line()
    across(w.y)
    for dy in range(1, mid):
        own.pass_mid(dy)
        across((w.y + dy) % mid)
    own.complete()

    def features(p):
        stacked = jnp.concatenate(
            [
                pool_ref[p, c, y * LINE + z].astype(F32).reshape(shard, count)
                for z in range(LINE)
                for y in range(mid)
                for c in range(2)
            ],
            axis=0,
        )
        scale = lax.rsqrt(jnp.mean(stacked * stacked, axis=0, keepdims=True) + 1e-06)
        return (stacked * scale).astype(BF16)

    feat = features(dp)
    proj = jnp.dot(feat.T, pairw_ref[...], preferred_element_type=F32).astype(BF16).astype(F32)
    rowp_ref[...] = proj[:, 0:head].reshape(rowp_ref.shape)
    col_wide = proj[:, head : 2 * head]
    w.landed(cot_in.at[pl.ds(0, n_seq - 1)], cot_recv)
    row_list = []
    for i in range(bins):
        row_list.append(jnp.sum(cot_ref[i].astype(F32) * col_wide, axis=0, keepdims=True))
    row_grad = jnp.concatenate(row_list, axis=0)
    col_grad = jnp.zeros((bins, head), F32)
    for p in range(n_seq):
        block = cot_in[p].astype(F32)
        for i in range(bins):
            col_grad = col_grad + block[i * bins : (i + 1) * bins] * rowp_ref[p, i : i + 1]
    grads[flat] = jnp.concatenate([row_grad, col_grad], axis=1).astype(BF16)
    grads_send, grads_recv = one(), one()

    def spread(k):
        peer = (flat + k + 1) % every
        w.send(
            grads.at[flat], grads.at[flat], grads_send, grads_recv, peer % n_seq, peer // n_seq
        )

    each(every - 1, spread)
    turned[dp] = feat
    for i in range(bins):
        pair_out[i] = (rowp_ref[me, i : i + 1] * col_wide).astype(BF16)
    for y in range(mid):
        for d in range(1, n_dp):
            other = (dp + d) % n_dp
            ref = group(other, core, y)
            w.landed(ref, group_recv.at[other, core, y])
            w.send(ref, ref, beside_send, group_recv.at[other, core, y], w.sibling)
    for d in range(1, n_dp):
        other = (dp + d) % n_dp
        for y in range(mid):
            w.landed(group(other, 1 - core, y), group_recv.at[other, 1 - core, y])
        turned[other] = features(other)
    w.landed(grads.at[pl.ds(0, every - 1)], grads_recv)

    w.landed(wkv_buf.at[pl.ds(0, n_seq - 1)], wkv_send)
    w.landed(wq_buf.at[pl.ds(0, n_seq - 1)], wq_send)
    for normed_send in normed_sends:
        w.landed(normed_ref.at[0, 0], normed_send)
    w.landed(q_ref.at[1], q_send)
    w.landed(wo_buf.at[0], wo_send)
    w.landed(kv_ref.at[0, pl.ds(0, chips - 1)], kv_sends[0])
    w.landed(kv_ref.at[0], kv_sends[1])
    w.landed(cot_in.at[pl.ds(0, n_seq - 1)], cot_send)
    for h in range(heads):
        w.landed(binned.at[h, pl.ds(0, chips - 1)], bin_send.at[h])
    w.landed(part_in, part_send)
    w.landed(pool_ref.at[0, 0, pl.ds(0, chips - 1)], own.send_sem.at[0])
    w.landed(pool_ref.at[0, 0], own.send_sem.at[1])
    w.landed(pool_ref.at[pl.ds(0, n_dp - 1), 0], across_send)
    w.landed(pool_ref.at[pl.ds(0, n_dp - 1), 0], beside_send)
    w.landed(grads.at[pl.ds(0, every - 1)], grads_send)


def tail_kernel(pair_ref, turned, grads, pair_hbm, grow_hbm, gcol_hbm, out_ref, sems):
    pair_copy = pltpu.make_async_copy(pair_ref, pair_hbm, sems.at[0])
    pair_copy.start()
    n_dp, width, count = turned.shape
    channels = grow_hbm.shape[1]
    whole = merge_rows(grads[...], n_dp * count)
    step = width // TAIL
    copies = [pair_copy]
    for k in range(TAIL):
        total = jnp.zeros((step, whole.shape[1]), F32)
        for p in range(n_dp):
            total = total + jnp.dot(
                turned[p, k * step : (k + 1) * step],
                whole[p * count : (p + 1) * count],
                preferred_element_type=F32,
            )
        total = total.astype(BF16)
        for c, target in enumerate((grow_hbm, gcol_hbm)):
            ref = out_ref.at[c, pl.ds(k * step, step)]
            ref[...] = total[:, c * channels : (c + 1) * channels]
            copy = pltpu.make_async_copy(
                ref, target.at[pl.ds(k * step, step)], sems.at[1 + 2 * k + c]
            )
            copy.start()
            copies.append(copy)
    for copy in copies:
        copy.wait()


def on_device(
    n_dp,
    n_seq,
    tokens,
    query_weight,
    key_weight,
    value_weight,
    output_weight,
    row_weight,
    col_weight,
    pair_cotangent,
):
    rows, width = tokens.shape[1:]
    shard, head = key_weight.shape
    heads_wide = query_weight.shape[1]
    half = heads_wide // 4
    bins, count, channels = pair_cotangent.shape[1:]
    third = shard // 3
    chips = n_seq // 2
    mid = chips // LINE
    vmem = pl.BlockSpec(memory_space=pltpu.VMEM)
    hbm = pl.BlockSpec(memory_space=pltpu.HBM)
    dma = pltpu.SemaphoreType.DMA
    every = n_dp * n_seq
    heads = 2 * half // head
    results = every * bins * 2 * channels + n_dp * width * count + bins * count * channels
    grant = 57 * 2**20 - 2 * results
    tail_grant = 16 * 2**20 if n_dp * count <= 512 else 44 * 2**20
    kept = pl.pallas_call(
        functools.partial(main_kernel, n_dp, n_seq),
        out_shape=(
            pltpu.VMEM((bins, count, channels), BF16),
            pltpu.VMEM((n_dp, width, count), BF16),
            pltpu.VMEM((every, bins, 2 * channels), BF16),
        ),
        in_specs=[hbm] * 8,
        out_specs=(vmem,) * 3,
        scratch_shapes=[
            pltpu.VMEM((n_seq, bins, channels), F32),
            pltpu.VMEM((rows, width), BF16),
            pltpu.VMEM((width, 2 * channels), BF16),
            pltpu.VMEM((bins, count, channels), BF16),
            pltpu.VMEM((n_seq, bins * bins, channels), BF16),
            pltpu.VMEM((n_seq, bins * bins, channels), BF16),
            pltpu.VMEM((2, 3, third, head), BF16),
            pltpu.VMEM((n_seq, 3, third, head), BF16),
            pltpu.VMEM((2, 3, third, half), BF16),
            pltpu.VMEM((n_seq, 3, third, half), BF16),
            pltpu.VMEM((2, 3, third, 2 * half), BF16),
            pltpu.VMEM((2, 3, third, 2 * half), BF16),
            pltpu.VMEM((2, 2, rows, width), BF16),
            pltpu.VMEM((3, 2 * rows, half), BF16),
            pltpu.VMEM((2, chips, 2 * rows, head), BF16),
            pltpu.VMEM((heads, chips, 2 * bins, head), BF16),
            pltpu.VMEM((2, shard, count), F32),
            pltpu.VMEM((shard, count), F32),
            pltpu.VMEM((n_dp, 2, chips, 3, third, count), BF16),
            dma((12,)),
            dma((n_seq,)),
            dma((n_seq,)),
            dma((n_seq,)),
            dma((heads,)),
            dma((heads,)),
            dma((n_seq,)),
            dma((n_dp, 2, mid)),
            dma((25,)),
        ],
        compiler_params=pltpu.CompilerParams(
            collective_id=0, has_side_effects=True, vmem_limit_bytes=grant
        ),
    )(
        tokens[0],
        query_weight.reshape(3, third, heads_wide),
        key_weight.reshape(3, third, head),
        value_weight.reshape(3, third, head),
        output_weight.reshape(3, third, heads_wide),
        row_weight,
        col_weight,
        pair_cotangent[0],
    )
    pair, grow, gcol = pl.pallas_call(
        tail_kernel,
        out_shape=(
            jax.ShapeDtypeStruct((bins, count, channels), BF16),
            jax.ShapeDtypeStruct((width, channels), BF16),
            jax.ShapeDtypeStruct((width, channels), BF16),
        ),
        in_specs=[vmem] * 3,
        out_specs=(hbm,) * 3,
        scratch_shapes=[pltpu.VMEM((2, width, channels), BF16), dma((1 + 2 * TAIL,))],
        compiler_params=pltpu.CompilerParams(vmem_limit_bytes=tail_grant),
    )(*kept)
    return (pair[None], grow, gcol)


def solution(mesh):
    placed = (
        P("dp", "seq", None),
        P("seq", None),
        P("seq", None),
        P("seq", None),
        P("seq", None),
        P(),
        P(),
        P("dp", "seq", None, None),
    )
    return jax.shard_map(
        functools.partial(on_device, mesh.shape["dp"], mesh.shape["seq"]),
        mesh=mesh,
        in_specs=placed,
        out_specs=(P("dp", "seq", None, None), P(), P()),
        check_vma=False,
    )
```

```python
import functools
import math

import jax
import jax.numpy as jnp
from jax import lax
from jax.experimental import pallas as pl
from jax.experimental.pallas import tpu as pltpu
from jax.sharding import PartitionSpec as P

POOL = 16
LINE = 4
TAIL = 3
ORDER = (1, LINE - 1, *range(2, LINE - 1))
F32 = jnp.float32
BF16 = jnp.bfloat16
MESH = pl.DeviceIdType.MESH
LAST = (((1,), (1,)), ((), ()))


def merge_rows(block, rows):
    if block.shape[1] % 16 == 0:
        return block.reshape(rows, block.shape[2])
    return block.astype(F32).reshape(rows, block.shape[2]).astype(block.dtype)


class Where:
    def __init__(self, n_dp, n_seq):
        self.n_dp, self.n_seq = n_dp, n_seq
        self.mid = n_seq // (LINE * 2)
        self.chips = n_seq // 2
        self.dp, self.me = lax.axis_index("dp"), lax.axis_index("seq")
        self.core = self.me % 2
        self.y = (self.me // 2) % self.mid
        self.z = self.me // (2 * self.mid)
        self.sibling = self.at(0, 0, True)

    def at(self, dz, dy, flip):
        z = (self.z + dz) % LINE
        y = (self.y + dy) % self.mid
        core = 1 - self.core if flip else self.core
        return (z * self.mid + y) * 2 + core

    def send(self, src, dst, send_sem, recv_sem, peer, dp=None):
        copy = pltpu.make_async_remote_copy(
            src_ref=src,
            dst_ref=dst,
            send_sem=send_sem,
            recv_sem=recv_sem,
            device_id=(self.dp if dp is None else dp, peer),
            device_id_type=MESH,
        )
        copy.start()

    def landed(self, ref, sem):
        pltpu.make_async_copy(ref, ref, sem).wait()


class Halves:
    def __init__(self, where, own, slot, send_sem, recv_sem):
        self.w, self.own, self.slot = where, own, slot
        self.send_sem, self.recv_sem = send_sem, recv_sem

    def give(self, peer, flip):
        w = self.w
        src = self.own(1 - w.core if flip else w.core)
        w.send(src, self.slot(w.me), self.send_sem, self.recv_sem.at[w.me], peer)

    def start_line(self):
        for dz in ORDER:
            for flip in (False, True):
                self.give(self.w.at(dz, 0, flip), flip)

    def start_mid(self):
        for dy in range(1, self.w.mid):
            for flip in (False, True):
                self.give(self.w.at(0, dy, flip), flip)

    def arrived(self, block):
        self.w.landed(self.slot(block), self.recv_sem.at[block])

    def pass_line(self):
        w = self.w
        for dz in ORDER:
            for flip in (False, True):
                block = w.at(dz, 0, flip)
                self.arrived(block)
                for dy in range(1, w.mid):
                    ref = self.slot(block)
                    w.send(ref, ref, self.send_sem, self.recv_sem.at[block], w.at(0, dy, False))

    def pass_mid(self):
        w = self.w
        for dz in (0, *ORDER):
            for dy in range(1, w.mid):
                for flip in (False, True):
                    block = w.at(dz, dy, flip)
                    self.arrived(block)


class Gather:
    def __init__(self, where, slot, send_sem, recv_sem):
        self.w, self.slot = where, slot
        self.send_sem, self.recv_sem = send_sem, recv_sem

    def push(self, block, peer, flip):
        ref = self.slot(block)
        sem = self.send_sem.at[1 if flip else 0]
        self.w.send(ref, ref, sem, self.recv_sem.at[block], peer)

    def arrived(self, block):
        self.w.landed(self.slot(block), self.recv_sem.at[block])

    def start(self):
        w = self.w
        for dz in ORDER:
            self.push(w.me, w.at(dz, 0, False), False)
        self.spread(0)

    def spread(self, dz):
        w = self.w
        block = w.at(dz, 0, False)
        for dy in range(1, w.mid):
            self.push(block, w.at(0, dy, False), False)
        self.push(block, w.sibling, True)

    def pass_line(self):
        for dz in ORDER:
            self.arrived(self.w.at(dz, 0, False))
            self.spread(dz)

    def pass_mid(self, dy):
        w = self.w
        for dz in (0, *ORDER):
            block = w.at(dz, dy, False)
            self.arrived(block)
            self.push(block, w.sibling, True)

    def complete(self):
        w = self.w
        for dz in (0, *ORDER):
            for dy in range(w.mid):
                self.arrived(w.at(dz, dy, True))


def each(total, act):
    def step(k, unused):
        act(k)
        return unused

    lax.fori_loop(0, total, step, 0)


def main_kernel(
    n_dp,
    n_seq,
    tok_hbm,
    wq_hbm,
    wk_hbm,
    wv_hbm,
    wo_hbm,
    roww_hbm,
    colw_hbm,
    cot_hbm,
    pair_out,
    turned,
    grads,
    rowp_ref,
    tok_ref,
    pairw_ref,
    cot_ref,
    pack,
    cot_in,
    wkv_own,
    wkv_buf,
    wq_own,
    wq_buf,
    wo_own,
    wo_buf,
    normed_ref,
    q_ref,
    kv_ref,
    binned,
    part_ref,
    part_in,
    pool_ref,
    load_sem,
    wkv_recv,
    wq_recv,
    kv_recv,
    bin_send,
    bin_recv,
    pool_recv,
    group_recv,
    sems,
):
    w = Where(n_dp, n_seq)
    dp, me, core, chips, mid = w.dp, w.me, w.core, w.chips, w.mid
    every = n_dp * n_seq
    flat = dp * n_seq + me
    head = wk_hbm.shape[2]
    half = wq_own.shape[3]
    heads = 2 * half // head
    rows, width = tok_ref.shape
    bins, count = cot_ref.shape[0:2]
    odd = dp % 2
    partner = dp + 1 - 2 * odd
    near = pl.multiple_of(odd * half, half)
    far = pl.multiple_of((1 - odd) * half, half)
    shard = width // n_seq
    sem = iter(range(sems.shape[0]))
    one = lambda: sems.at[next(sem)]

    sources = [
        (wk_hbm, wkv_own.at[0]),
        (wv_hbm, wkv_own.at[1]),
        (wq_hbm.at[:, :, pl.ds(near, half)], wq_own.at[0]),
        (wq_hbm.at[:, :, pl.ds(2 * half + near, half)], wq_own.at[1]),
        (tok_hbm, tok_ref),
        (wo_hbm.at[:, :, pl.ds(near, half)], wo_own.at[0, :, :, pl.ds(0, half)]),
        (wo_hbm.at[:, :, pl.ds(far, half)], wo_own.at[0, :, :, pl.ds(half, half)]),
        (wo_hbm.at[:, :, pl.ds(2 * half + near, half)], wo_own.at[1, :, :, pl.ds(0, half)]),
        (wo_hbm.at[:, :, pl.ds(2 * half + far, half)], wo_own.at[1, :, :, pl.ds(half, half)]),
        (cot_hbm, cot_ref),
        (roww_hbm, pairw_ref.at[:, pl.ds(0, head)]),
        (colw_hbm, pairw_ref.at[:, pl.ds(head, head)]),
    ]
    loads = [
        pltpu.make_async_copy(src, dst, load_sem.at[i]) for i, (src, dst) in enumerate(sources)
    ]
    for load in loads:
        load.start()

    barrier = pltpu.get_barrier_semaphore()

    def greet(peer, p):
        pl.semaphore_signal(barrier, inc=1, device_id=(p, peer), device_id_type=MESH)

    if n_dp > 2:

        def greet_next(k):
            peer = (flat + k + 1) % every
            greet(peer % n_seq, peer // n_seq)

        each(every - 1, greet_next)
        met = every - 1
    else:
        near_by = [w.sibling]
        for flip in (False, True):
            near_by += [w.at(dz, 0, flip) for dz in ORDER]
            near_by += [w.at(0, dy, flip) for dy in range(1, mid)]
        for peer in near_by:
            greet(peer, dp)
        for d in range(1, n_dp):
            greet(me, (dp + d) % n_dp)
        met = len(near_by) + n_dp - 1
    loads[4].wait()
    tok = tok_ref[...].astype(F32)
    normed_ref[0, core] = (
        tok * lax.rsqrt(jnp.mean(tok * tok, axis=1, keepdims=True) + 1e-06)
    ).astype(BF16)
    for load in loads[0:4]:
        load.wait()

    wkv_send, wq_send = one(), one()
    wkv = Halves(w, lambda c: wkv_own.at[c], lambda s: wkv_buf.at[s], wkv_send, wkv_recv)
    wq = Halves(w, lambda c: wq_own.at[c], lambda s: wq_buf.at[s], wq_send, wq_recv)

    def repack():
        loads[9].wait()
        squares = cot_ref[...].astype(F32)
        for p in range(n_seq):
            pack[p] = jnp.concatenate(
                [squares[i, p * bins : (p + 1) * bins] for i in range(bins)], axis=0
            ).astype(BF16)
        cot_in[me] = pack[me]

    pl.semaphore_wait(barrier, met)
    across_recv = one()
    mine = normed_ref.at[0, core]
    normed_sends = one(), one(), one()
    w.send(mine, normed_ref.at[1, core], normed_sends[0], across_recv, me, partner)
    normed_recv, beside_recv = one(), one()
    w.send(mine, mine, normed_sends[1], normed_recv, w.sibling)
    wkv.start_line()
    wkv.start_mid()
    wkv.give(w.sibling, True)
    wq.start_line()
    wq.give(w.sibling, True)
    wq.start_mid()
    wkv_buf[me] = wkv_own[core]
    wq_buf[me] = wq_own[core]
    repack()
    wkv.pass_line()
    for load in loads[5:9]:
        load.wait()
    wo_send, wo_recv = one(), one()
    w.send(wo_own.at[1 - core], wo_buf.at[core], wo_send, wo_recv, w.sibling)
    wo_buf[core] = wo_own[core]
    w.landed(normed_ref.at[0, 1 - core], normed_recv)
    normed = normed_ref[0].reshape(2 * rows, width)
    wkv.pass_mid()
    wkv.arrived(w.sibling)

    def whole(buf):
        return merge_rows(
            buf[...].reshape(n_seq * buf.shape[1], buf.shape[2], buf.shape[3]), width
        )

    cot_send, cot_recv = one(), one()

    def turn(k):
        peer = (me + k + 1) % n_seq
        w.send(pack.at[peer], cot_in.at[me], cot_send, cot_recv, peer)


    kv_ref[core, me // 2] = jnp.dot(
        normed, whole(wkv_buf), preferred_element_type=F32
    ).astype(BF16)
    kv_sends = (one(), one())

    class Sends:
        def __init__(self, pair):
            self.at = pair

    blocks = Gather(w, lambda s: kv_ref.at[s % 2, s // 2], Sends(kv_sends), kv_recv)
    blocks.start()
    wq.pass_line()
    blocks.pass_line()
    other = normed_ref.at[1, core]
    w.landed(other, across_recv)
    w.send(other, other, normed_sends[2], beside_recv, w.sibling)
    wq.pass_mid()
    wq.arrived(w.sibling)
    w.landed(normed_ref.at[1, 1 - core], beside_recv)
    wq_all = whole(wq_buf)
    q_ref[2] = jnp.dot(
        normed_ref[1].reshape(2 * rows, width), wq_all, preferred_element_type=F32
    ).astype(BF16)
    q_send, q_recv = one(), one()
    w.send(q_ref.at[2], q_ref.at[1], q_send, q_recv, me, partner)
    q_ref[0] = jnp.dot(normed, wq_all, preferred_element_type=F32).astype(BF16)
    for dy in range(1, mid):
        blocks.pass_mid(dy)
    blocks.complete()

    keys = kv_ref[0].reshape(n_seq * rows, head)
    values = kv_ref[1].reshape(n_seq * rows, head)
    factor = math.log2(math.e) / math.sqrt(head)
    chip_bins = 2 * bins
    per = half // head
    for h in range(heads):
        if h == per:
            w.landed(q_ref.at[1], q_recv)
        queries = q_ref[h // per, :, h % per * head : (h % per + 1) * head]
        scores = lax.dot_general(queries, keys, LAST, preferred_element_type=F32)
        top = jnp.max(scores, axis=1, keepdims=True)
        weights = jnp.exp2((scores - top) * factor)
        total = jnp.sum(weights, axis=1, keepdims=True)
        out = jnp.dot(weights.astype(BF16), values, preferred_element_type=F32) / total
        out = out.astype(BF16).astype(F32)
        binned[h, me // 2] = jnp.sum(out.reshape(chip_bins, POOL, head), axis=1).astype(BF16)
        ref = binned.at[h, me // 2]
        for dy in range(mid):
            for dz in (2, 1, 3, 0):
                if dz or dy:
                    w.send(ref, ref, bin_send.at[h], bin_recv.at[h], w.at(dz, dy, False))

    each(n_seq - 1, turn)
    for load in loads[10:]:
        load.wait()
    w.landed(wo_buf.at[1 - core], wo_recv)
    wo = merge_rows(
        wo_buf[...].reshape(2 * wo_buf.shape[1], wo_buf.shape[2], 2 * half), 2 * shard
    )
    partial = jnp.zeros((2 * shard, count), F32)
    for h in range(heads):
        w.landed(binned.at[h, pl.ds(0, chips - 1)], bin_recv.at[h])
        partial = partial + lax.dot_general(
            wo[:, h * head : (h + 1) * head],
            binned[h].reshape(count, head),
            LAST,
            preferred_element_type=F32,
        )
    part_ref[0] = partial[0:shard]
    part_ref[1] = partial[shard : 2 * shard]
    part_send, part_recv = one(), one()
    w.send(part_ref.at[1 - core], part_in, part_send, part_recv, w.sibling)
    w.landed(part_in, part_recv)
    pooled = (part_ref[core] + part_in[...]) * (1.0 / POOL)
    spot = lambda s: ((s // 2) % mid) * LINE + s // (2 * mid)
    pool_ref[dp, core, spot(me)] = pooled.reshape(pool_ref.shape[3:]).astype(BF16)
    own = Gather(
        w, lambda s: pool_ref.at[dp, s % 2, spot(s)], Sends((one(), one())), pool_recv
    )
    own.start()
    across_send, beside_send = one(), one()

    def group(p, c, y):
        return pool_ref.at[p, c, pl.ds(y * LINE, LINE)]

    def across(y):
        for d in range(1, n_dp):
            ref = group(dp, core, y)
            w.send(ref, ref, across_send, group_recv.at[dp, core, y], me, (dp + d) % n_dp)

    own.pass_line()
    across(w.y)
    for dy in range(1, mid):
        own.pass_mid(dy)
        across((w.y + dy) % mid)
    own.complete()

    def features(p):
        stacked = jnp.concatenate(
            [
                pool_ref[p, c, y * LINE + z].astype(F32).reshape(shard, count)
                for z in range(LINE)
                for y in range(mid)
                for c in range(2)
            ],
            axis=0,
        )
        scale = lax.rsqrt(jnp.mean(stacked * stacked, axis=0, keepdims=True) + 1e-06)
        return (stacked * scale).astype(BF16)

    feat = features(dp)
    proj = jnp.dot(feat.T, pairw_ref[...], preferred_element_type=F32).astype(BF16).astype(F32)
    rowp_ref[...] = proj[:, 0:head].reshape(rowp_ref.shape)
    col_wide = proj[:, head : 2 * head]
    w.landed(cot_in.at[pl.ds(0, n_seq - 1)], cot_recv)
    row_list = []
    for i in range(bins):
        row_list.append(jnp.sum(cot_ref[i].astype(F32) * col_wide, axis=0, keepdims=True))
    row_grad = jnp.concatenate(row_list, axis=0)
    col_grad = jnp.zeros((bins, head), F32)
    for p in range(n_seq):
        block = cot_in[p].astype(F32)
        for i in range(bins):
            col_grad = col_grad + block[i * bins : (i + 1) * bins] * rowp_ref[p, i : i + 1]
    grads[flat] = jnp.concatenate([row_grad, col_grad], axis=1).astype(BF16)
    grads_send, grads_recv = one(), one()

    def spread(k):
        peer = (flat + k + 1) % every
        w.send(
            grads.at[flat], grads.at[flat], grads_send, grads_recv, peer % n_seq, peer // n_seq
        )

    each(every - 1, spread)
    turned[dp] = feat
    for i in range(bins):
        pair_out[i] = (rowp_ref[me, i : i + 1] * col_wide).astype(BF16)
    for y in range(mid):
        for d in range(1, n_dp):
            other = (dp + d) % n_dp
            ref = group(other, core, y)
            w.landed(ref, group_recv.at[other, core, y])
            w.send(ref, ref, beside_send, group_recv.at[other, core, y], w.sibling)
    for d in range(1, n_dp):
        other = (dp + d) % n_dp
        for y in range(mid):
            w.landed(group(other, 1 - core, y), group_recv.at[other, 1 - core, y])
        turned[other] = features(other)

    w.landed(wkv_buf.at[pl.ds(0, n_seq - 1)], wkv_send)
    w.landed(wq_buf.at[pl.ds(0, n_seq - 1)], wq_send)
    for normed_send in normed_sends:
        w.landed(normed_ref.at[0, 0], normed_send)
    w.landed(q_ref.at[1], q_send)
    w.landed(wo_buf.at[0], wo_send)
    w.landed(kv_ref.at[0, pl.ds(0, chips - 1)], kv_sends[0])
    w.landed(kv_ref.at[0], kv_sends[1])
    w.landed(cot_in.at[pl.ds(0, n_seq - 1)], cot_send)
    for h in range(heads):
        w.landed(binned.at[h, pl.ds(0, chips - 1)], bin_send.at[h])
    w.landed(part_in, part_send)
    w.landed(pool_ref.at[0, 0, pl.ds(0, chips - 1)], own.send_sem.at[0])
    w.landed(pool_ref.at[0, 0], own.send_sem.at[1])
    w.landed(pool_ref.at[pl.ds(0, n_dp - 1), 0], across_send)
    w.landed(pool_ref.at[pl.ds(0, n_dp - 1), 0], beside_send)
    w.landed(grads.at[pl.ds(0, every - 1)], grads_send)
    w.landed(grads.at[pl.ds(0, every - 1)], grads_recv)


def tail_kernel(pair_ref, turned, grads, pair_hbm, grow_hbm, gcol_hbm, out_ref, sems):
    pair_copy = pltpu.make_async_copy(pair_ref, pair_hbm, sems.at[0])
    pair_copy.start()
    n_dp, width, count = turned.shape
    channels = grow_hbm.shape[1]
    whole = merge_rows(grads[...], n_dp * count)
    step = width // TAIL
    copies = [pair_copy]
    for k in range(TAIL):
        total = jnp.zeros((step, whole.shape[1]), F32)
        for p in range(n_dp):
            total = total + jnp.dot(
                turned[p, k * step : (k + 1) * step],
                whole[p * count : (p + 1) * count],
                preferred_element_type=F32,
            )
        total = total.astype(BF16)
        for c, target in enumerate((grow_hbm, gcol_hbm)):
            ref = out_ref.at[c, pl.ds(k * step, step)]
            ref[...] = total[:, c * channels : (c + 1) * channels]
            copy = pltpu.make_async_copy(
                ref, target.at[pl.ds(k * step, step)], sems.at[1 + 2 * k + c]
            )
            copy.start()
            copies.append(copy)
    for copy in copies:
        copy.wait()


def on_device(
    n_dp,
    n_seq,
    tokens,
    query_weight,
    key_weight,
    value_weight,
    output_weight,
    row_weight,
    col_weight,
    pair_cotangent,
):
    rows, width = tokens.shape[1:]
    shard, head = key_weight.shape
    heads_wide = query_weight.shape[1]
    half = heads_wide // 4
    bins, count, channels = pair_cotangent.shape[1:]
    third = shard // 3
    chips = n_seq // 2
    mid = chips // LINE
    vmem = pl.BlockSpec(memory_space=pltpu.VMEM)
    hbm = pl.BlockSpec(memory_space=pltpu.HBM)
    dma = pltpu.SemaphoreType.DMA
    every = n_dp * n_seq
    heads = 2 * half // head
    results = every * bins * 2 * channels + n_dp * width * count + bins * count * channels
    grant = 57 * 2**20 - 2 * results
    tail_grant = 16 * 2**20 if n_dp * count <= 512 else 44 * 2**20
    kept = pl.pallas_call(
        functools.partial(main_kernel, n_dp, n_seq),
        out_shape=(
            pltpu.VMEM((bins, count, channels), BF16),
            pltpu.VMEM((n_dp, width, count), BF16),
            pltpu.VMEM((every, bins, 2 * channels), BF16),
        ),
        in_specs=[hbm] * 8,
        out_specs=(vmem,) * 3,
        scratch_shapes=[
            pltpu.VMEM((n_seq, bins, channels), F32),
            pltpu.VMEM((rows, width), BF16),
            pltpu.VMEM((width, 2 * channels), BF16),
            pltpu.VMEM((bins, count, channels), BF16),
            pltpu.VMEM((n_seq, bins * bins, channels), BF16),
            pltpu.VMEM((n_seq, bins * bins, channels), BF16),
            pltpu.VMEM((2, 3, third, head), BF16),
            pltpu.VMEM((n_seq, 3, third, head), BF16),
            pltpu.VMEM((2, 3, third, half), BF16),
            pltpu.VMEM((n_seq, 3, third, half), BF16),
            pltpu.VMEM((2, 3, third, 2 * half), BF16),
            pltpu.VMEM((2, 3, third, 2 * half), BF16),
            pltpu.VMEM((2, 2, rows, width), BF16),
            pltpu.VMEM((3, 2 * rows, half), BF16),
            pltpu.VMEM((2, chips, 2 * rows, head), BF16),
            pltpu.VMEM((heads, chips, 2 * bins, head), BF16),
            pltpu.VMEM((2, shard, count), F32),
            pltpu.VMEM((shard, count), F32),
            pltpu.VMEM((n_dp, 2, chips, 3, third, count), BF16),
            dma((12,)),
            dma((n_seq,)),
            dma((n_seq,)),
            dma((n_seq,)),
            dma((heads,)),
            dma((heads,)),
            dma((n_seq,)),
            dma((n_dp, 2, mid)),
            dma((25,)),
        ],
        compiler_params=pltpu.CompilerParams(
            collective_id=0, has_side_effects=True, vmem_limit_bytes=grant
        ),
    )(
        tokens[0],
        query_weight.reshape(3, third, heads_wide),
        key_weight.reshape(3, third, head),
        value_weight.reshape(3, third, head),
        output_weight.reshape(3, third, heads_wide),
        row_weight,
        col_weight,
        pair_cotangent[0],
    )
    pair, grow, gcol = pl.pallas_call(
        tail_kernel,
        out_shape=(
            jax.ShapeDtypeStruct((bins, count, channels), BF16),
            jax.ShapeDtypeStruct((width, channels), BF16),
            jax.ShapeDtypeStruct((width, channels), BF16),
        ),
        in_specs=[vmem] * 3,
        out_specs=(hbm,) * 3,
        scratch_shapes=[pltpu.VMEM((2, width, channels), BF16), dma((1 + 2 * TAIL,))],
        compiler_params=pltpu.CompilerParams(vmem_limit_bytes=tail_grant),
    )(*kept)
    return (pair[None], grow, gcol)


def solution(mesh):
    placed = (
        P("dp", "seq", None),
        P("seq", None),
        P("seq", None),
        P("seq", None),
        P("seq", None),
        P(),
        P(),
        P("dp", "seq", None, None),
    )
    return jax.shard_map(
        functools.partial(on_device, mesh.shape["dp"], mesh.shape["seq"]),
        mesh=mesh,
        in_specs=placed,
        out_specs=(P("dp", "seq", None, None), P(), P()),
        check_vma=False,
    )
```
